512 devices in a mesh: leaf: 64 (over z, y), sep: 8 (over x, core).
Axes of the slice: x: 4, y: 8, z: 8, core: 2. Of those that a mesh axis runs over, the one named last changes fastest.
Arguments:
- shot_columns: float32 [64, 8, 1536, 256], P('leaf', 'sep'), may hold values from -6 to 6
- factor_tiles: bfloat16 [64, 8, 12, 4, 128, 128], P('leaf', 'sep'), may hold values from -0.25 to 0.25
- factor_cols: int32 [64, 8, 12, 4], P('leaf', 'sep'), may hold values from 0 to 11, all different within a row
- boundary_rows: int32 [64, 8, 64], P('leaf', 'sep'), may hold values from 0 to 1535
- boundary_map: int32 [64, 8, 64], P('leaf', 'sep'), may hold values from 0 to 2047
- boundary_count: int32 [64, 8], P('leaf', 'sep'), may hold values from 16 to 64, as said below
- separator_load: float32 [8, 2048, 256], P('sep', 'leaf'), may hold values from -6 to 6
- inverse_tiles: bfloat16 [8, 2048, 8, 4, 128], P(None, 'leaf', 'sep'), may hold values from -0.09375 to 0.09375
- inverse_cols: int32 [8, 64, 8, 4], P(None, 'leaf', 'sep'), may hold values from 0 to 15, all different within a row
Outputs:
- leaf_solution: float32 [64, 8, 1536, 256], P('leaf', 'sep')
- separator_solution: float32 [8, 2048, 256], P('sep', 'leaf')
The draws below stay inside these ranges and needn't reach their ends.
Inputs may be any that keep to these rules, and one draw needn't show every extreme that they name: `boundary_count`: some leaf section has exactly 64 live boundary rows in every draw.
All inputs are finite; a program needn't handle non-finite values.
Results may differ from the reference program's by a relative error of at most 0.0036.
Values may be sent and summed in bfloat16 or wider, within the bound.
No kernel may reach another device: no remote copies, remote signals or barrier semaphores. Data moves between devices by JAX's collectives and lax.ppermute only.
A program may use at most 64 MiB of HBM per device.

```python
import jax
import jax.numpy as jnp
from jax import lax

NS = 16384
TILE = 128
LEAF_DEV = 1536
COLS = 256
TPR = 4
KMAX = 64
TR = 12
SEP_DEV = 2048
STRIP = 32
TC = 16
NZ = 4
N_LEAF = 64
N_SEP = 8


def draw_boundary_count(key, part):
    key_counts = jax.random.fold_in(key, 11)
    key_where = jax.random.fold_in(key, 23)
    counts = jax.random.randint(key_counts, (N_LEAF * N_SEP,), KMAX // 4, KMAX + 1)
    chosen = jax.random.randint(key_where, (), 0, N_LEAF * N_SEP)
    counts = jnp.where(jnp.arange(N_LEAF * N_SEP) == chosen, KMAX, counts)
    return counts.reshape(N_LEAF, N_SEP).astype(jnp.int32)


def set_ends(result, own_key, low, top_value):
    spot = [jax.random.randint(jax.random.fold_in(own_key, axis), (), 0, length) for axis, length in enumerate(result.shape)]
    longest = result.shape.index(max(result.shape))
    beside = spot[:longest] + [(spot[longest] + 1) % result.shape[longest]] + spot[longest + 1:]
    return result.at[tuple(spot)].set(low).at[tuple(beside)].set(top_value)


def level_of(rng, extent, pieces, smallest, top_value):
    level = 1.0
    for dim, blocks in pieces:
        steps = jax.random.uniform(jax.random.fold_in(jax.random.fold_in(rng, 6), dim), (blocks,), jnp.float32, smallest / len(pieces), top_value / len(pieces))
        level = level * jnp.repeat(jnp.exp(steps), extent[dim] // blocks).reshape((-1,) + (1,) * (len(extent) - 1 - dim))
    return level


def different_ones(own_key, rows, count, top, lift):
    order = jax.random.permutation(jax.random.fold_in(own_key, 1), count)
    pull = order
    for power in range(3):
        pull = pull * pull // count
    pull = pull * lift // count
    tickets = jax.random.randint(jax.random.fold_in(own_key, 2), (rows, count), 0, 4096) + pull
    holders = jax.random.permutation(jax.random.fold_in(own_key, 3), rows)[jnp.arange(count) % rows]
    tickets = jnp.where(jnp.arange(rows)[:, None] == holders[None, :], 1 << 14, tickets)
    score = tickets * count + jnp.arange(count)
    return lax.top_k(score.astype(jnp.int32), top)[1].astype(jnp.int32)


def gaussian(rng, extent, spread, limit, shards=(), held_as=jnp.bfloat16):
    array = spread * jax.random.normal(rng, extent, jnp.float32)
    if shards:
        array = array * level_of(rng, extent, shards, -0.22, 0.18)
    return jnp.clip(array, -limit, limit).astype(held_as)


def setup_inputs(seed: int = 0) -> dict:
    key_list = jax.random.split(jax.random.key(seed), 10)
    shot_columns = gaussian(key_list[0], (N_LEAF, N_SEP, LEAF_DEV, COLS), 1.0, 6.0, ((0, 64), (1, 8)), jnp.float32)
    factor_tiles = gaussian(key_list[1], (N_LEAF, N_SEP, TR, TPR, TILE, TILE), (TPR * TILE) ** -0.5, 0.25, ((0, 64), (1, 8)))
    factor_cols = different_ones(key_list[2], N_LEAF * N_SEP * TR, LEAF_DEV // TILE, TPR, 0).reshape((N_LEAF, N_SEP, TR, TPR))
    boundary_rows = set_ends(jax.random.randint(key_list[3], (N_LEAF, N_SEP, KMAX), 0, LEAF_DEV), jax.random.fold_in(key_list[3], 1), 0, LEAF_DEV - 1).astype(jnp.int32)
    boundary_map = set_ends(jax.random.randint(key_list[4], (N_LEAF, N_SEP, KMAX), 0, NS // N_SEP), jax.random.fold_in(key_list[4], 1), 0, (NS // N_SEP) - 1).astype(jnp.int32)
    boundary_count = draw_boundary_count(jax.random.fold_in(key_list[9], 71), 0)
    separator_load = gaussian(key_list[6], (N_SEP, SEP_DEV, COLS), 1.0, 6.0, ((0, 8), (1, 64)), jnp.float32)
    inverse_tiles = gaussian(key_list[7], (N_SEP, SEP_DEV, N_SEP, NZ, TILE), (N_SEP * NZ * TILE) ** -0.5, 0.09375, ((1, 64), (2, 8)))
    inverse_cols = different_ones(key_list[8], N_SEP * N_LEAF * N_SEP, NS // N_SEP // TILE, NZ, 0).reshape((N_SEP, N_LEAF, N_SEP, NZ))
    return dict(shot_columns=shot_columns, factor_tiles=factor_tiles, factor_cols=factor_cols, boundary_rows=boundary_rows, boundary_map=boundary_map, boundary_count=boundary_count, separator_load=separator_load, inverse_tiles=inverse_tiles, inverse_cols=inverse_cols)


def forward_tiles(tiles, tile_cols, vector):
    width = vector.shape[-1]
    tiled_rows = vector.astype(jnp.bfloat16).reshape(-1, TILE, width)
    picked = tiled_rows[tile_cols]
    product = jnp.einsum("tkab,tkbn->tan", tiles.astype(jnp.float32), picked.astype(jnp.float32))
    return product.reshape(-1, width)


def flipped_tile_grid(tiles, tile_cols, vector):
    width = vector.shape[-1]
    count_rows = tiles.shape[0]
    tiled_rows = vector.astype(jnp.bfloat16).reshape(count_rows, TILE, width)
    addend_tiles = jnp.einsum("tkab,tan->tkbn", tiles.astype(jnp.float32), tiled_rows.astype(jnp.float32))
    reduced_total = jax.ops.segment_sum(addend_tiles.reshape(-1, TILE, width), tile_cols.reshape(-1).astype(jnp.int32), num_segments=count_rows)
    return reduced_total.reshape(-1, width)


def reference(shot_columns, factor_tiles, factor_cols, boundary_rows, boundary_map, boundary_count, separator_load, inverse_tiles, inverse_cols):
    sections = N_LEAF * N_SEP
    flat_shots = shot_columns.reshape(sections, LEAF_DEV, COLS)
    flat_tiles = factor_tiles.reshape(sections, TR, TPR, TILE, TILE)
    flat_cols = factor_cols.reshape(sections, TR, TPR)
    forward = lax.map(lambda item: forward_tiles(item[1], item[2], item[0]), (flat_shots, flat_tiles, flat_cols))
    forward = forward.reshape(N_LEAF, N_SEP, LEAF_DEV, COLS)
    live_mask = jnp.arange(KMAX, dtype=jnp.int32)[None, None, :] < boundary_count[:, :, None]
    boundary_values = jax.vmap(jax.vmap(lambda block, rows: block[rows]))(forward, boundary_rows)
    boundary_values = jnp.where(live_mask[:, :, :, None], boundary_values, jnp.float32(0.0))
    per_section = jnp.transpose(boundary_values, (1, 0, 2, 3)).reshape(N_SEP, N_LEAF * KMAX, COLS)
    section_map = jnp.transpose(boundary_map, (1, 0, 2)).reshape(N_SEP, N_LEAF * KMAX)
    coupled = jax.vmap(lambda values, desired_output: jax.ops.segment_sum(values, desired_output, num_segments=SEP_DEV))(per_section, section_map)
    residual = separator_load - coupled
    column_tiles = residual.astype(jnp.bfloat16).reshape(N_SEP, TC, TILE, COLS)
    strip_tiles = inverse_tiles.reshape(N_SEP * N_LEAF, STRIP, N_SEP, NZ, TILE)
    strip_cols = inverse_cols.reshape(N_SEP * N_LEAF, N_SEP, NZ)

    def apply_strip(item):
        tiles, chosen = item
        picked = jax.vmap(lambda block, index: block[index])(column_tiles, chosen)
        return jnp.einsum("iskc,skcn->in", tiles.astype(jnp.float32), picked.astype(jnp.float32))

    solved_unknowns = lax.map(apply_strip, (strip_tiles, strip_cols)).reshape(N_SEP, SEP_DEV, COLS)
    needed = jax.vmap(lambda maps: jax.vmap(lambda block, index: block[index])(solved_unknowns, maps))(boundary_map)
    needed = jnp.where(live_mask[:, :, :, None], needed, jnp.float32(0.0))
    corrected = jax.vmap(jax.vmap(lambda block, rows, terms: block.at[rows].add(-terms)))(forward, boundary_rows, needed)
    flattened_adjusted = corrected.reshape(sections, LEAF_DEV, COLS)
    leaf_solution = lax.map(lambda item: flipped_tile_grid(item[1], item[2], item[0]), (flattened_adjusted, flat_tiles, flat_cols))
    return leaf_solution.reshape(N_LEAF, N_SEP, LEAF_DEV, COLS), solved_unknowns
```

```python
import functools

import jax
import jax.numpy as jnp
from jax import lax
from jax.experimental import pallas as pl
from jax.experimental.pallas import tpu as pltpu
from jax.sharding import Mesh, PartitionSpec as P

TILE = 128
HI_SHIFT = 7
DEAD = 255
MAP_ROWS = 8
F32 = jnp.float32
BF16 = jnp.bfloat16

SMEM = functools.partial(pl.BlockSpec, memory_space=pltpu.SMEM)
VMEM = functools.partial(pl.BlockSpec, memory_space=pltpu.VMEM)


def call(kernel, out_shape, in_specs, scratch=()):
    single = not isinstance(out_shape, (tuple, list))
    return pl.pallas_call(
        kernel,
        out_shape=out_shape,
        in_specs=in_specs,
        out_specs=VMEM() if single else tuple(VMEM() for _ in out_shape),
        scratch_shapes=list(scratch),
    )


def exchange(value, axes):
    return lax.all_to_all(value, axes, split_axis=0, concat_axis=0, tiled=True)


def forward_kernel(cols, rows, count, shots, tiles, own_map, forward, sent, rounded, picked):
    count_rows, per_row = tiles.shape[0], tiles.shape[1]
    peers, _, width = sent.shape
    kmax = picked.shape[0] - MAP_ROWS
    rounded[...] = shots[...].astype(BF16)
    for t in range(count_rows):
        total = None
        for k in range(0, per_row, 2):
            left = jnp.concatenate([tiles[t, k], tiles[t, k + 1]], axis=1)
            starts = [pl.multiple_of(cols[t, k + i] * TILE, TILE) for i in range(2)]
            right = jnp.concatenate([rounded[pl.ds(s, TILE), :] for s in starts], axis=0)
            term = jnp.dot(left, right, preferred_element_type=F32)
            total = term if total is None else total + term
        forward[pl.ds(t * TILE, TILE), :] = total
    live = count[0, 0]
    for k in range(kmax):
        row = forward[pl.ds(rows[0, k], 1), :]
        picked[pl.ds(k, 1), :] = jnp.where(k < live, row, 0.0)
    target = own_map[...]
    lane = lax.broadcasted_iota(jnp.int32, target.shape, 1)
    high = jnp.where(lane < live, target >> HI_SHIFT, DEAD).astype(F32)
    low = (target & (TILE - 1)).astype(F32)
    picked[pl.ds(kmax, MAP_ROWS), :] = jnp.zeros((MAP_ROWS, width), F32)
    picked[pl.ds(kmax, 1), pl.ds(0, kmax)] = high
    picked[pl.ds(kmax + 1, 1), pl.ds(0, kmax)] = low
    whole = picked[...].astype(BF16)
    for p in range(peers):
        sent[p] = whole


def combine_kernel(got, partial, chosen, *, n_y, strip):
    y = lax.axis_index("y")
    peers, held, width = got.shape
    kmax = held - MAP_ROWS
    n_rows = chosen.shape[0]
    r = lax.broadcasted_iota(jnp.int32, (n_rows, kmax), 0)
    row_id = ((r // strip) * n_y + y) * strip + r % strip
    row_id = row_id.astype(F32)
    total = None
    for p in range(peers):
        targets = got[p, pl.ds(kmax, MAP_ROWS), :].astype(F32)[:, :kmax]
        target = targets[0:1] * float(TILE) + targets[1:2]
        hot = jnp.where(row_id == target, 1.0, 0.0).astype(BF16)
        chosen[:, pl.ds(p * kmax, kmax)] = hot
        term = jnp.dot(hot, got[p, pl.ds(0, kmax), :], preferred_element_type=F32)
        total = term if total is None else total + term
    partial[...] = total.reshape(partial.shape)


def residual_kernel(load, got, sent):
    total = got[0]
    for p in range(1, got.shape[0]):
        total = total + got[p]
    value = (load[...] - total).astype(BF16)
    for p in range(sent.shape[0]):
        sent[p] = value


def separator_kernel(cols, strips, residual, product):
    sections, per_row = cols.shape
    for q in range(sections):
        total = None
        for k in range(0, per_row, 2):
            starts = [pl.multiple_of(cols[q, k + i] * TILE, TILE) for i in range(2)]
            right = jnp.concatenate([residual[pl.ds(s, TILE), :] for s in starts], axis=0)
            term = jnp.dot(strips[q, :, pl.ds(k * TILE, 2 * TILE)], right, preferred_element_type=F32)
            total = term if total is None else total + term
        product[q] = total


def solution_kernel(got, own, sent):
    total = got[0]
    for p in range(1, got.shape[0]):
        total = total + got[p]
    own[...] = total
    value = total.astype(BF16)
    for p in range(sent.shape[0]):
        sent[p] = value


def pick_kernel(chosen, strips, sent):
    peers, kmax, width = sent.shape
    picked = lax.dot_general(chosen[...], strips[...], (((0,), (0,)), ((), ())), preferred_element_type=F32)
    sent[...] = picked.astype(BF16).reshape(peers, kmax, width)


def transposed_kernel(cols, rows, got, forward, tiles, out, corrected, needed):
    count_rows, per_row = tiles.shape[0], tiles.shape[1]
    peers, kmax, width = got.shape
    total = got[0].astype(F32)
    for p in range(1, peers):
        total = total + got[p].astype(F32)
    needed[...] = total
    corrected[...] = forward[...]
    for k in range(kmax):
        at = pl.ds(rows[0, k], 1)
        corrected[at, :] = corrected[at, :] - needed[pl.ds(k, 1), :]
    out[...] = jnp.zeros_like(out)
    for t in range(count_rows):
        block = corrected[pl.ds(t * TILE, TILE), :].astype(BF16)
        for k in range(per_row):
            term = lax.dot_general(tiles[t, k], block, (((0,), (0,)), ((), ())), preferred_element_type=F32)
            at = pl.ds(pl.multiple_of(cols[t, k] * TILE, TILE), TILE)
            out[at, :] = out[at, :] + term


def body(
    shot_columns,
    factor_tiles,
    factor_cols,
    boundary_rows,
    boundary_map,
    boundary_count,
    separator_load,
    inverse_tiles,
    inverse_cols,
):
    n_z, n_y = lax.axis_size("z"), lax.axis_size("y")
    n_sep = lax.axis_size("sep")
    shots, tiles, cols = shot_columns[0, 0], factor_tiles[0, 0], factor_cols[0, 0]
    rows, own_map, load = boundary_rows[0], boundary_map[0], separator_load[0]
    leaf_rows, width = shots.shape
    kmax = rows.shape[1]
    strip = load.shape[0]
    shape = jax.ShapeDtypeStruct
    forward, sent = call(
        forward_kernel,
        (shape((leaf_rows, width), F32), shape((n_y, kmax + MAP_ROWS, width), BF16)),
        [SMEM(), SMEM(), SMEM(), VMEM(), VMEM(), VMEM()],
        [pltpu.VMEM((leaf_rows, width), BF16), pltpu.VMEM((kmax + MAP_ROWS, width), F32)],
    )(cols, rows, boundary_count, shots, tiles, own_map)
    got = exchange(sent, "y")
    partial, chosen = call(
        functools.partial(combine_kernel, n_y=n_y, strip=strip),
        (shape((n_z, strip, width), F32), shape((n_z * strip, n_y * kmax), BF16)),
        [VMEM()],
    )(got)
    got = exchange(partial, "z")
    sent = call(residual_kernel, shape((n_z * n_y, strip, width), BF16), [VMEM(), VMEM()])(load, got)
    residual = exchange(sent, ("z", "y")).reshape(-1, width)
    strips = inverse_tiles[:, :, 0].reshape(n_sep, strip, -1)
    product = call(separator_kernel, shape((n_sep, strip, width), F32), [SMEM(), VMEM(), VMEM()])(
        inverse_cols[:, 0, 0], strips, residual
    )
    got = exchange(product, "sep")
    own, sent = call(
        solution_kernel, (shape((strip, width), F32), shape((n_z, strip, width), BF16)), [VMEM()]
    )(got)
    solved = exchange(sent, "z").reshape(-1, width)
    sent = call(pick_kernel, shape((n_y, kmax, width), BF16), [VMEM(), VMEM()])(chosen, solved)
    got = exchange(sent, "y")
    leaf_solution = call(
        transposed_kernel,
        shape((leaf_rows, width), F32),
        [SMEM(), SMEM(), VMEM(), VMEM(), VMEM()],
        [pltpu.VMEM((leaf_rows, width), F32), pltpu.VMEM((kmax, width), F32)],
    )(cols, rows, got, forward, tiles)
    return leaf_solution[None, None], own[None]


def solution(mesh):
    n_leaf, n_sep = mesh.shape["leaf"], mesh.shape["sep"]
    n_y = 8
    torus = Mesh(mesh.devices.reshape(n_leaf // n_y, n_y, n_sep), ("z", "y", "sep"))
    leaf = ("z", "y")
    placed = (
        P(leaf, "sep", None, None),
        P(leaf, "sep", None, None, None, None),
        P(leaf, "sep", None, None),
        P(leaf, "sep", None),
        P(leaf, "sep", None),
        P(leaf, "sep"),
        P("sep", leaf, None),
        P(None, leaf, "sep", None, None),
        P(None, leaf, "sep", None),
    )
    return jax.shard_map(
        body,
        mesh=torus,
        in_specs=placed,
        out_specs=(P(leaf, "sep", None, None), P("sep", leaf, None)),
        check_vma=False,
    )
```

```python
import functools

import jax
import jax.numpy as jnp
from jax import lax
from jax.experimental import pallas as pl
from jax.experimental.pallas import tpu as pltpu
from jax.sharding import Mesh, PartitionSpec as P

TILE = 128
SHIFT = 7
DEAD = 255
SLOTS = 8
EXTRA = 8
F32 = jnp.float32
BF16 = jnp.bfloat16

SMEM = functools.partial(pl.BlockSpec, memory_space=pltpu.SMEM)
VMEM = functools.partial(pl.BlockSpec, memory_space=pltpu.VMEM)


def near(value):
    return pltpu.with_memory_space_constraint(value, pltpu.VMEM)


def call(kernel, out_shape, in_specs, scratch=(), out_specs=None):
    single = not isinstance(out_shape, (tuple, list))
    if out_specs is None:
        out_specs = VMEM() if single else tuple(VMEM() for _ in out_shape)
    return pl.pallas_call(
        kernel,
        out_shape=out_shape,
        in_specs=in_specs,
        out_specs=out_specs,
        scratch_shapes=list(scratch),
    )


def exchange(value, axes):
    return lax.all_to_all(value, axes, split_axis=0, concat_axis=0, tiled=True)


def over_rows(left, right):
    return lax.dot_general(left, right, (((0,), (0,)), ((), ())), preferred_element_type=F32)


def over_lanes(left, right):
    return lax.dot_general(left, right, (((1,), (1,)), ((), ())), preferred_element_type=F32)


def forward_kernel(
    cols, rows, targets, count, shots, tiles, own_map,
    forward, sent, taken, slots,
    rounded, exact, picked, filled, *, strip,
):
    count_rows, per_row = tiles.shape[0], tiles.shape[1]
    peers, _, width = sent.shape
    kmax = taken.shape[0]
    rounded[...] = shots[...].astype(BF16)
    for t in range(count_rows):
        total = None
        for k in range(0, per_row, 2):
            left = jnp.concatenate([tiles[t, k], tiles[t, k + 1]], axis=1)
            starts = [pl.multiple_of(cols[k + i, t] * TILE, TILE) for i in range(2)]
            right = jnp.concatenate([rounded[pl.ds(s, TILE), :] for s in starts], axis=0)
            term = jnp.dot(left, right, preferred_element_type=F32)
            total = term if total is None else total + term
        exact[pl.ds(t * TILE, TILE), :] = total
        forward[pl.ds(t * TILE, TILE), :] = total.astype(BF16)
    live = count[0, 0]
    for s in range(filled.shape[0]):
        filled[s] = 0
    lane = lax.broadcasted_iota(jnp.int32, own_map.shape, 1)
    place = jnp.zeros(own_map.shape, jnp.int32)
    most = 0
    for k in range(kmax):
        row = exact[pl.ds(rows[0, k], 1), :]
        taken[pl.ds(k, 1), :] = row
        picked[pl.ds(k, 1), :] = jnp.where(k < live, row, 0.0)
        owner = targets[0, k] // strip
        slot = filled[owner]
        alive = (k < live).astype(jnp.int32)
        filled[owner] = slot + alive
        most = jnp.maximum(most, alive * (slot + 1))
        place = jnp.where(lane == k, slot, place)
        slots[0, k] = jnp.where(k < live, owner * SLOTS + jnp.minimum(slot, SLOTS - 1), -1)
    target = own_map[...]
    high = jnp.where(lane < live, target >> SHIFT, DEAD).astype(F32)
    low = (target & (TILE - 1)).astype(F32)
    picked[pl.ds(kmax, EXTRA), :] = jnp.zeros((EXTRA, width), F32)
    picked[pl.ds(kmax, 1), pl.ds(0, kmax)] = high
    picked[pl.ds(kmax + 1, 1), pl.ds(0, kmax)] = low
    picked[pl.ds(kmax + 2, 1), pl.ds(0, kmax)] = place.astype(F32)
    over = jnp.where(most > SLOTS, 1.0, 0.0)
    picked[pl.ds(kmax + 3, 1), :] = jnp.full((1, width), over, F32)
    whole = picked[...].astype(BF16)
    for p in range(peers):
        sent[p] = whole


def ring_targets(got, n_rows, n_y, strip):
    y = lax.axis_index("y")
    kmax = got.shape[1] - EXTRA
    r = lax.broadcasted_iota(jnp.int32, (n_rows, kmax), 0)
    row_id = ((r // strip) * n_y + y) * strip + r % strip
    row_id = row_id.astype(F32)
    for p in range(got.shape[0]):
        info = got[p, pl.ds(kmax, EXTRA), :].astype(F32)
        target = info[0:1, :kmax] * float(TILE) + info[1:2, :kmax]
        yield p, info, jnp.where(row_id == target, 1.0, 0.0).astype(BF16)


def combine_kernel(got, sent, *, n_y, strip):
    peers, _, width = got.shape
    n_z = sent.shape[0]
    kmax = got.shape[1] - EXTRA
    total, wanted, over = None, [], None
    for p, info, hot in ring_targets(got, n_z * strip, n_y, strip):
        term = jnp.dot(hot, got[p, pl.ds(0, kmax), :], preferred_element_type=F32)
        total = term if total is None else total + term
        slot = lax.broadcasted_iota(jnp.int32, (TILE, kmax), 0)
        place = info[2:3, :kmax].astype(jnp.int32)
        mine = jnp.where(slot == place + p * SLOTS, 1.0, 0.0)
        mine = jnp.where(place < SLOTS, mine, 0.0).astype(BF16)
        wanted.append(over_lanes(hot, mine))
        flag = info[3:4, :TILE]
        over = flag if over is None else jnp.maximum(over, flag)
    asked = wanted[0]
    for w in wanted[1:]:
        asked = asked + w
    lane = lax.broadcasted_iota(jnp.int32, asked.shape, 1)
    asked = jnp.where(lane < peers * SLOTS, asked, jnp.broadcast_to(over, asked.shape))
    sent[:, :, pl.ds(0, width)] = total.astype(BF16).reshape(n_z, strip, width)
    sent[:, :, pl.ds(width, TILE)] = asked.astype(BF16).reshape(n_z, strip, TILE)


def residual_kernel(load, got, sent):
    width = load.shape[1]
    total = got[0, :, pl.ds(0, width)].astype(F32)
    for p in range(1, got.shape[0]):
        total = total + got[p, :, pl.ds(0, width)].astype(F32)
    value = (load[...] - total).astype(BF16)
    for p in range(sent.shape[0]):
        sent[p] = value


def separator_kernel(cols, strips, residual, got, product):
    per_row, sections = cols.shape
    _, strip, width = residual.shape
    per_tile = TILE // strip
    for q in range(sections):
        total = None
        for k in range(0, per_row, 2):
            right = jnp.concatenate(
                [
                    residual[pl.ds(cols[k + i, q] * per_tile, per_tile)].reshape(TILE, width)
                    for i in range(2)
                ],
                axis=0,
            )
            term = jnp.dot(strips[q, :, pl.ds(k * TILE, 2 * TILE)], right, preferred_element_type=F32)
            total = term if total is None else total + term
        product[q, pl.ds(0, strip), :] = total
    over = got[0, pl.ds(0, EXTRA), pl.ds(width, TILE)].astype(F32)
    for p in range(1, got.shape[0]):
        over = jnp.maximum(over, got[p, pl.ds(0, EXTRA), pl.ds(width, TILE)].astype(F32))
    over = jnp.concatenate([over] * (width // TILE), axis=1)
    for q in range(sections):
        product[q, pl.ds(strip, EXTRA), :] = over


def solution_kernel(got, asked, own, sent, over):
    strip, width = own.shape
    total = got[0]
    for p in range(1, got.shape[0]):
        total = total + got[p]
    own[...] = total[:strip]
    most = got[0, pl.ds(strip, EXTRA), pl.ds(0, TILE)]
    for p in range(1, got.shape[0]):
        most = jnp.maximum(most, got[p, pl.ds(strip, EXTRA), pl.ds(0, TILE)])
    over[...] = most
    value = total[:strip].astype(BF16)
    n_z = asked.shape[0]
    per = sent.shape[0] // n_z
    for p in range(n_z):
        rows = over_rows(asked[p, :, pl.ds(width, TILE)], value)[: per * SLOTS]
        sent[pl.ds(p * per, per)] = rows.astype(BF16).reshape(per, SLOTS, width)


def pick_kernel(got, strips, sent, *, n_y, strip):
    n_rows = strips.shape[0]
    for p, _, hot in ring_targets(got, n_rows, n_y, strip):
        sent[p] = over_rows(hot, strips[...]).astype(BF16)


def transposed_kernel(cols, count, forward, tiles, row_lanes, base, reach, same, wide):
    count_rows, per_row = tiles.shape[0], tiles.shape[1]
    leaf_rows, width = forward.shape
    kmax = same.shape[0]
    wide[...] = jnp.zeros_like(wide)
    lanes = row_lanes[...]
    sums = None
    for t in range(count_rows):
        r = lax.broadcasted_iota(jnp.int32, (TILE, TILE), 0) + t * TILE
        hot = jnp.where(r == lanes, 1.0, 0.0).astype(BF16)
        term = over_rows(hot, hot)
        sums = term if sums is None else sums + term
        block = jnp.concatenate([forward[pl.ds(t * TILE, TILE), :], hot], axis=1)
        for k in range(per_row):
            at = pl.ds(pl.multiple_of(cols[k, t] * TILE, TILE), TILE)
            wide[at, :] = wide[at, :] + over_rows(tiles[t, k], block)
    base[...] = wide[:, pl.ds(0, width)]
    reach[...] = wide[:, pl.ds(width, TILE)].astype(BF16)
    same[...] = sums[:kmax]


def finish(needed, count, taken, same, base, reach, out, change):
    @pl.when(pl.program_id(0) == 0)
    def _():
        kmax = taken.shape[0]
        equal = same[...][:, :kmax]
        k = lax.broadcasted_iota(jnp.int32, equal.shape, 1)
        mine = lax.broadcasted_iota(jnp.int32, equal.shape, 0)
        earlier = jnp.sum(jnp.where(k < mine, equal, 0.0), axis=1, keepdims=True)
        live = jnp.where(k < count[0, 0], equal, 0.0).astype(BF16)
        term = jnp.dot(live, needed().astype(BF16), preferred_element_type=F32)
        before = taken[...]
        delta = (before - term).astype(BF16).astype(F32) - before.astype(BF16).astype(F32)
        delta = jnp.where(earlier == 0.0, delta, 0.0)
        high = delta.astype(BF16)
        change[pl.ds(0, kmax), :] = high
        change[pl.ds(kmax, kmax), :] = (delta - high.astype(F32)).astype(BF16)

    out[...] = base[...] + jnp.dot(reach[...], change[...], preferred_element_type=F32)


def slot_finish_kernel(slots, count, got, taken, same, base, reach, out, change, plain, rows):
    kmax = taken.shape[0]

    def needed():
        plain[...] = got[...].reshape(plain.shape).astype(F32)
        for k in range(kmax):
            at = slots[0, k]
            row = plain[pl.ds(jnp.maximum(at, 0), 1), :]
            rows[pl.ds(k, 1), :] = jnp.where(at >= 0, row, 0.0)
        return rows[...]

    finish(needed, count, taken, same, base, reach, out, change)


def ring_finish_kernel(count, got, taken, same, base, reach, out, change):
    def needed():
        total = got[0].astype(F32)
        for p in range(1, got.shape[0]):
            total = total + got[p].astype(F32)
        return total

    finish(needed, count, taken, same, base, reach, out, change)


def body(
    shot_columns,
    factor_tiles,
    factor_cols,
    boundary_rows,
    boundary_map,
    boundary_count,
    separator_load,
    inverse_tiles,
    inverse_cols,
):
    n_z, n_y = lax.axis_size("z"), lax.axis_size("y")
    n_sep, n_leaf = lax.axis_size("sep"), n_z * n_y
    shots, tiles, cols = shot_columns[0, 0], factor_tiles[0, 0], factor_cols[0, 0].T
    rows, own_map, load = boundary_rows[0], boundary_map[0], separator_load[0]
    leaf_rows, width = shots.shape
    kmax = rows.shape[1]
    strip = load.shape[0]
    shape = jax.ShapeDtypeStruct
    forward, sent, taken, slots = call(
        functools.partial(forward_kernel, strip=strip),
        (
            shape((leaf_rows, width), BF16),
            shape((n_y, kmax + EXTRA, width), BF16),
            shape((kmax, width), F32),
            shape((1, kmax), jnp.int32),
        ),
        [SMEM(), SMEM(), SMEM(), SMEM(), VMEM(), VMEM(), VMEM()],
        [
            pltpu.VMEM((leaf_rows, width), BF16),
            pltpu.VMEM((leaf_rows, width), F32),
            pltpu.VMEM((kmax + EXTRA, width), F32),
            pltpu.SMEM((n_leaf,), jnp.int32),
        ],
        (VMEM(), VMEM(), VMEM(), SMEM()),
    )(cols, rows, own_map, boundary_count, shots, tiles, own_map)
    ring = exchange(sent, "y")
    sent = call(
        functools.partial(combine_kernel, n_y=n_y, strip=strip),
        shape((n_z, strip, width + TILE), BF16),
        [VMEM()],
    )(near(ring))
    asked = exchange(sent, "z")
    sent = call(residual_kernel, shape((n_leaf, strip, width), BF16), [VMEM(), VMEM()])(load, near(asked))
    residual = exchange(sent, ("z", "y"))
    held_rows, _ = lax.optimization_barrier((rows, asked[0, 0, 0]))
    base, reach, same = call(
        transposed_kernel,
        (shape((leaf_rows, width), F32), shape((leaf_rows, TILE), BF16), shape((kmax, TILE), F32)),
        [SMEM(), SMEM(), VMEM(), VMEM(), VMEM()],
        [pltpu.VMEM((leaf_rows, width + TILE), F32)],
    )(cols, boundary_count, forward, tiles, jnp.concatenate([held_rows, held_rows], axis=1))
    strips = inverse_tiles[:, :, 0].reshape(n_sep, strip, -1)
    product = call(
        separator_kernel,
        shape((n_sep, strip + EXTRA, width), F32),
        [SMEM(), VMEM(), VMEM(), VMEM()],
    )(inverse_cols[:, 0, 0].T, near(strips), near(residual), near(asked))
    got = exchange(product, "sep")
    own, sent, over = call(
        solution_kernel,
        (shape((strip, width), F32), shape((n_leaf, SLOTS, width), BF16), shape((EXTRA, TILE), F32)),
        [VMEM(), VMEM()],
    )(near(got), near(asked))

    pieces = 4
    part = leaf_rows // pieces
    whole = lambda *dims: pl.BlockSpec(dims, lambda i: (0,) * len(dims))
    tail = [
        whole(kmax, width),
        whole(kmax, TILE),
        pl.BlockSpec((part, width), lambda i: (i, 0)),
        pl.BlockSpec((part, TILE), lambda i: (i, 0)),
    ]

    def finished(kernel, lead, scratch):
        return pl.pallas_call(
            kernel,
            grid=(pieces,),
            out_shape=shape((leaf_rows, width), F32),
            in_specs=lead + tail,
            out_specs=pl.BlockSpec((part, width), lambda i: (i, 0)),
            scratch_shapes=[pltpu.VMEM((2 * kmax, width), BF16)] + scratch,
        )

    def by_slots():
        got = exchange(sent, ("z", "y"))
        return finished(
            slot_finish_kernel,
            [SMEM(), SMEM(), whole(n_leaf, SLOTS, width)],
            [pltpu.VMEM((n_leaf * SLOTS, width), F32), pltpu.VMEM((kmax, width), F32)],
        )(slots, boundary_count, got, taken, same, base, reach)

    def by_rings():
        value = jnp.broadcast_to(own.astype(BF16)[None], (n_z, strip, width))
        solved = exchange(value, "z").reshape(-1, width)
        picked = call(
            functools.partial(pick_kernel, n_y=n_y, strip=strip),
            shape((n_y, kmax, width), BF16),
            [VMEM(), VMEM()],
        )(ring, solved)
        got = exchange(picked, "y")
        return finished(ring_finish_kernel, [SMEM(), whole(n_y, kmax, width)], [])(
            boundary_count, got, taken, same, base, reach
        )

    leaf_solution = lax.cond(jnp.max(over) > 0.0, by_rings, by_slots)
    return leaf_solution[None, None], own[None]


def solution(mesh):
    n_leaf, n_sep = mesh.shape["leaf"], mesh.shape["sep"]
    n_y = 8
    torus = Mesh(mesh.devices.reshape(n_leaf // n_y, n_y, n_sep), ("z", "y", "sep"))
    leaf = ("z", "y")
    placed = (
        P(leaf, "sep", None, None),
        P(leaf, "sep", None, None, None, None),
        P(leaf, "sep", None, None),
        P(leaf, "sep", None),
        P(leaf, "sep", None),
        P(leaf, "sep"),
        P("sep", leaf, None),
        P(None, leaf, "sep", None, None),
        P(None, leaf, "sep", None),
    )
    return jax.shard_map(
        body,
        mesh=torus,
        in_specs=placed,
        out_specs=(P(leaf, "sep", None, None), P("sep", leaf, None)),
        check_vma=False,
    )
```

```python
import functools

import jax
import jax.numpy as jnp
from jax import lax
from jax.experimental import pallas as pl
from jax.experimental.pallas import tpu as pltpu
from jax.sharding import Mesh, PartitionSpec as P

TILE = 128
SHIFT = 7
DEAD = 255
SLOTS = 8
EXTRA = 8
F32 = jnp.float32
BF16 = jnp.bfloat16

SMEM = functools.partial(pl.BlockSpec, memory_space=pltpu.SMEM)
VMEM = functools.partial(pl.BlockSpec, memory_space=pltpu.VMEM)


def near(value):
    return pltpu.with_memory_space_constraint(value, pltpu.VMEM)


def call(kernel, out_shape, in_specs, scratch=(), out_specs=None):
    single = not isinstance(out_shape, (tuple, list))
    if out_specs is None:
        out_specs = VMEM() if single else tuple(VMEM() for _ in out_shape)
    return pl.pallas_call(
        kernel,
        out_shape=out_shape,
        in_specs=in_specs,
        out_specs=out_specs,
        scratch_shapes=list(scratch),
    )


def exchange(value, axes):
    return lax.all_to_all(value, axes, split_axis=0, concat_axis=0, tiled=True)


def over_rows(left, right):
    return lax.dot_general(left, right, (((0,), (0,)), ((), ())), preferred_element_type=F32)


def over_lanes(left, right):
    return lax.dot_general(left, right, (((1,), (1,)), ((), ())), preferred_element_type=F32)


def forward_kernel(
    cols, rows, targets, count, shots, tiles, own_map,
    forward, sent, taken, slots,
    rounded, exact, picked, filled, *, strip,
):
    count_rows, per_row = tiles.shape[0], tiles.shape[1]
    peers, _, width = sent.shape
    kmax = taken.shape[0]
    rounded[...] = shots[...].astype(BF16)
    for t in range(count_rows):
        total = None
        for k in range(0, per_row, 2):
            left = jnp.concatenate([tiles[t, k], tiles[t, k + 1]], axis=1)
            starts = [pl.multiple_of(cols[k + i, t] * TILE, TILE) for i in range(2)]
            right = jnp.concatenate([rounded[pl.ds(s, TILE), :] for s in starts], axis=0)
            term = jnp.dot(left, right, preferred_element_type=F32)
            total = term if total is None else total + term
        exact[pl.ds(t * TILE, TILE), :] = total
        forward[pl.ds(t * TILE, TILE), :] = total.astype(BF16)
    live = count[0, 0]
    for s in range(filled.shape[0]):
        filled[s] = 0
    lane = lax.broadcasted_iota(jnp.int32, own_map.shape, 1)
    place = jnp.zeros(own_map.shape, jnp.int32)
    most = 0
    for k in range(kmax):
        row = exact[pl.ds(rows[0, k], 1), :]
        taken[pl.ds(k, 1), :] = row
        picked[pl.ds(k, 1), :] = jnp.where(k < live, row, 0.0)
        owner = targets[0, k] // strip
        slot = filled[owner]
        alive = (k < live).astype(jnp.int32)
        filled[owner] = slot + alive
        most = jnp.maximum(most, alive * (slot + 1))
        place = jnp.where(lane == k, slot, place)
        slots[0, k] = jnp.where(k < live, owner * SLOTS + jnp.minimum(slot, SLOTS - 1), -1)
    target = own_map[...]
    high = jnp.where(lane < live, target >> SHIFT, DEAD).astype(F32)
    low = (target & (TILE - 1)).astype(F32)
    picked[pl.ds(kmax, EXTRA), :] = jnp.zeros((EXTRA, width), F32)
    picked[pl.ds(kmax, 1), pl.ds(0, kmax)] = high
    picked[pl.ds(kmax + 1, 1), pl.ds(0, kmax)] = low
    picked[pl.ds(kmax + 2, 1), pl.ds(0, kmax)] = place.astype(F32)
    over = jnp.where(most > SLOTS, 1.0, 0.0)
    picked[pl.ds(kmax + 3, 1), :] = jnp.full((1, width), over, F32)
    whole = picked[...].astype(BF16)
    for p in range(peers):
        sent[p] = whole


def ring_targets(got, n_rows, n_y, strip):
    y = lax.axis_index("y")
    kmax = got.shape[1] - EXTRA
    r = lax.broadcasted_iota(jnp.int32, (n_rows, kmax), 0)
    row_id = ((r // strip) * n_y + y) * strip + r % strip
    row_id = row_id.astype(F32)
    for p in range(got.shape[0]):
        info = got[p, pl.ds(kmax, EXTRA), :].astype(F32)
        target = info[0:1, :kmax] * float(TILE) + info[1:2, :kmax]
        yield p, info, jnp.where(row_id == target, 1.0, 0.0).astype(BF16)


def combine_kernel(got, sent, *, n_y, strip):
    peers, _, width = got.shape
    n_z = sent.shape[0]
    kmax = got.shape[1] - EXTRA
    total, wanted, over = None, [], None
    for p, info, hot in ring_targets(got, n_z * strip, n_y, strip):
        term = jnp.dot(hot, got[p, pl.ds(0, kmax), :], preferred_element_type=F32)
        total = term if total is None else total + term
        slot = lax.broadcasted_iota(jnp.int32, (TILE, kmax), 0)
        place = info[2:3, :kmax].astype(jnp.int32)
        mine = jnp.where(slot == place + p * SLOTS, 1.0, 0.0)
        mine = jnp.where(place < SLOTS, mine, 0.0).astype(BF16)
        wanted.append(over_lanes(hot, mine))
        flag = info[3:4, :TILE]
        over = flag if over is None else jnp.maximum(over, flag)
    asked = wanted[0]
    for w in wanted[1:]:
        asked = asked + w
    lane = lax.broadcasted_iota(jnp.int32, asked.shape, 1)
    asked = jnp.where(lane < peers * SLOTS, asked, jnp.broadcast_to(over, asked.shape))
    sent[:, :, pl.ds(0, width)] = total.astype(BF16).reshape(n_z, strip, width)
    sent[:, :, pl.ds(width, TILE)] = asked.astype(BF16).reshape(n_z, strip, TILE)


def residual_kernel(load, got, sent):
    width = load.shape[1]
    total = got[0, :, pl.ds(0, width)].astype(F32)
    for p in range(1, got.shape[0]):
        total = total + got[p, :, pl.ds(0, width)].astype(F32)
    value = (load[...] - total).astype(BF16)
    for p in range(sent.shape[0]):
        sent[p] = value


def separator_kernel(cols, strips, residual, got, product):
    per_row, sections = cols.shape
    _, strip, width = residual.shape
    per_tile = TILE // strip
    for q in range(sections):
        total = None
        for k in range(0, per_row, 2):
            right = jnp.concatenate(
                [
                    residual[pl.ds(cols[k + i, q] * per_tile, per_tile)].reshape(TILE, width)
                    for i in range(2)
                ],
                axis=0,
            )
            term = jnp.dot(strips[q, :, pl.ds(k * TILE, 2 * TILE)], right, preferred_element_type=F32)
            total = term if total is None else total + term
        product[q, pl.ds(0, strip), :] = total
    over = got[0, pl.ds(0, EXTRA), pl.ds(width, TILE)].astype(F32)
    for p in range(1, got.shape[0]):
        over = jnp.maximum(over, got[p, pl.ds(0, EXTRA), pl.ds(width, TILE)].astype(F32))
    over = jnp.concatenate([over] * (width // TILE), axis=1)
    for q in range(sections):
        product[q, pl.ds(strip, EXTRA), :] = over


def solution_kernel(got, asked, own, sent, over):
    strip, width = own.shape
    total = got[0]
    for p in range(1, got.shape[0]):
        total = total + got[p]
    own[...] = total[:strip]
    most = got[0, pl.ds(strip, EXTRA), pl.ds(0, TILE)]
    for p in range(1, got.shape[0]):
        most = jnp.maximum(most, got[p, pl.ds(strip, EXTRA), pl.ds(0, TILE)])
    lane = lax.broadcasted_iota(jnp.int32, most.shape, 1)
    over[0, 0] = (jnp.max(jnp.where(lane == TILE - 1, most, 0.0)) > 0.0).astype(jnp.int32)
    value = total[:strip].astype(BF16)
    n_z = asked.shape[0]
    per = sent.shape[0] // n_z
    for p in range(n_z):
        rows = over_rows(asked[p, :, pl.ds(width, TILE)], value)[: per * SLOTS]
        sent[pl.ds(p * per, per)] = rows.astype(BF16).reshape(per, SLOTS, width)


def pick_kernel(got, strips, sent, *, n_y, strip):
    n_rows = strips.shape[0]
    for p, _, hot in ring_targets(got, n_rows, n_y, strip):
        sent[p] = over_rows(hot, strips[...]).astype(BF16)


def transposed_kernel(cols, count, forward, tiles, row_lanes, base, reach, same, wide):
    count_rows, per_row = tiles.shape[0], tiles.shape[1]
    leaf_rows, width = forward.shape
    kmax = same.shape[0]
    wide[...] = jnp.zeros_like(wide)
    lanes = row_lanes[...]
    sums = None
    for t in range(count_rows):
        r = lax.broadcasted_iota(jnp.int32, (TILE, TILE), 0) + t * TILE
        hot = jnp.where(r == lanes, 1.0, 0.0).astype(BF16)
        term = over_rows(hot, hot)
        sums = term if sums is None else sums + term
        block = jnp.concatenate([forward[pl.ds(t * TILE, TILE), :], hot], axis=1)
        for k in range(per_row):
            at = pl.ds(pl.multiple_of(cols[k, t] * TILE, TILE), TILE)
            wide[at, :] = wide[at, :] + over_rows(tiles[t, k], block)
    base[...] = wide[:, pl.ds(0, width)]
    reach[...] = wide[:, pl.ds(width, TILE)].astype(BF16)
    same[...] = sums[:kmax]


def finish(needed, count, taken, same, base, reach, out, change):
    kmax = taken.shape[0]
    equal = same[...][:, :kmax]
    k = lax.broadcasted_iota(jnp.int32, equal.shape, 1)
    mine = lax.broadcasted_iota(jnp.int32, equal.shape, 0)
    earlier = jnp.sum(jnp.where(k < mine, equal, 0.0), axis=1, keepdims=True)
    live = jnp.where(k < count[0, 0], equal, 0.0).astype(BF16)
    term = jnp.dot(live, needed().astype(BF16), preferred_element_type=F32)
    before = taken[...]
    delta = (before - term).astype(BF16).astype(F32) - before.astype(BF16).astype(F32)
    delta = jnp.where(earlier == 0.0, delta, 0.0)
    high = delta.astype(BF16)
    change[pl.ds(0, kmax), :] = high
    change[pl.ds(kmax, kmax), :] = (delta - high.astype(F32)).astype(BF16)
    out[...] = base[...] + jnp.dot(reach[...], change[...], preferred_element_type=F32)


def slot_finish_kernel(slots, count, got, taken, same, base, reach, out, change, plain, rows):
    kmax = taken.shape[0]

    def needed():
        plain[...] = got[...].reshape(plain.shape).astype(F32)
        for k in range(kmax):
            at = slots[0, k]
            row = plain[pl.ds(jnp.maximum(at, 0), 1), :]
            rows[pl.ds(k, 1), :] = jnp.where(at >= 0, row, 0.0)
        return rows[...]

    finish(needed, count, taken, same, base, reach, out, change)


def ring_finish_kernel(count, got, taken, same, base, reach, out, change):
    def needed():
        total = got[0].astype(F32)
        for p in range(1, got.shape[0]):
            total = total + got[p].astype(F32)
        return total

    finish(needed, count, taken, same, base, reach, out, change)


def body(
    shot_columns,
    factor_tiles,
    factor_cols,
    boundary_rows,
    boundary_map,
    boundary_count,
    separator_load,
    inverse_tiles,
    inverse_cols,
):
    n_z, n_y = lax.axis_size("z"), lax.axis_size("y")
    n_sep, n_leaf = lax.axis_size("sep"), n_z * n_y
    shots, tiles, cols = shot_columns[0, 0], factor_tiles[0, 0], factor_cols[0, 0].T
    rows, own_map, load = boundary_rows[0], boundary_map[0], separator_load[0]
    leaf_rows, width = shots.shape
    kmax = rows.shape[1]
    strip = load.shape[0]
    shape = jax.ShapeDtypeStruct
    forward, sent, taken, slots = call(
        functools.partial(forward_kernel, strip=strip),
        (
            shape((leaf_rows, width), BF16),
            shape((n_y, kmax + EXTRA, width), BF16),
            shape((kmax, width), F32),
            shape((1, kmax), jnp.int32),
        ),
        [SMEM(), SMEM(), SMEM(), SMEM(), VMEM(), VMEM(), VMEM()],
        [
            pltpu.VMEM((leaf_rows, width), BF16),
            pltpu.VMEM((leaf_rows, width), F32),
            pltpu.VMEM((kmax + EXTRA, width), F32),
            pltpu.SMEM((n_leaf,), jnp.int32),
        ],
        (VMEM(), VMEM(), VMEM(), SMEM()),
    )(cols, rows, own_map, boundary_count, shots, tiles, own_map)
    ring = exchange(sent, "y")
    sent = call(
        functools.partial(combine_kernel, n_y=n_y, strip=strip),
        shape((n_z, strip, width + TILE), BF16),
        [VMEM()],
    )(near(ring))
    asked = exchange(sent, "z")
    sent = call(residual_kernel, shape((n_leaf, strip, width), BF16), [VMEM(), VMEM()])(load, near(asked))
    residual = exchange(sent, ("z", "y"))
    held_rows, _ = lax.optimization_barrier((rows, asked[0, 0, 0]))
    base, reach, same = call(
        transposed_kernel,
        (shape((leaf_rows, width), F32), shape((leaf_rows, TILE), BF16), shape((kmax, TILE), F32)),
        [SMEM(), SMEM(), VMEM(), VMEM(), VMEM()],
        [pltpu.VMEM((leaf_rows, width + TILE), F32)],
    )(cols, boundary_count, forward, tiles, jnp.concatenate([held_rows, held_rows], axis=1))
    strips = inverse_tiles[:, :, 0].reshape(n_sep, strip, -1)
    product = call(
        separator_kernel,
        shape((n_sep, strip + EXTRA, width), F32),
        [SMEM(), VMEM(), VMEM(), VMEM()],
    )(inverse_cols[:, 0, 0].T, near(strips), near(residual), near(asked))
    got = exchange(product, "sep")
    own, sent, over = call(
        solution_kernel,
        (shape((strip, width), F32), shape((n_leaf, SLOTS, width), BF16), shape((1, 1), jnp.int32)),
        [VMEM(), VMEM()],
        out_specs=(VMEM(), VMEM(), SMEM()),
    )(near(got), near(asked))

    def finished(kernel, lead, scratch):
        return call(
            kernel,
            shape((leaf_rows, width), F32),
            lead + [VMEM(), VMEM(), VMEM(), VMEM()],
            [pltpu.VMEM((2 * kmax, width), BF16)] + scratch,
        )

    def by_slots():
        got = exchange(sent, ("z", "y"))
        return finished(
            slot_finish_kernel,
            [SMEM(), SMEM(), VMEM()],
            [pltpu.VMEM((n_leaf * SLOTS, width), F32), pltpu.VMEM((kmax, width), F32)],
        )(slots, boundary_count, near(got), taken, same, near(base), near(reach))

    def by_rings():
        value = jnp.broadcast_to(own.astype(BF16)[None], (n_z, strip, width))
        solved = exchange(value, "z").reshape(-1, width)
        picked = call(
            functools.partial(pick_kernel, n_y=n_y, strip=strip),
            shape((n_y, kmax, width), BF16),
            [VMEM(), VMEM()],
        )(ring, solved)
        got = exchange(picked, "y")
        return finished(ring_finish_kernel, [SMEM(), VMEM()], [])(
            boundary_count, near(got), taken, same, near(base), near(reach)
        )

    leaf_solution = lax.cond(over[0, 0] > 0, by_rings, by_slots)
    return leaf_solution[None, None], own[None]


def solution(mesh):
    n_leaf, n_sep = mesh.shape["leaf"], mesh.shape["sep"]
    n_y = 8
    torus = Mesh(mesh.devices.reshape(n_leaf // n_y, n_y, n_sep), ("z", "y", "sep"))
    leaf = ("z", "y")
    placed = (
        P(leaf, "sep", None, None),
        P(leaf, "sep", None, None, None, None),
        P(leaf, "sep", None, None),
        P(leaf, "sep", None),
        P(leaf, "sep", None),
        P(leaf, "sep"),
        P("sep", leaf, None),
        P(None, leaf, "sep", None, None),
        P(None, leaf, "sep", None),
    )
    return jax.shard_map(
        body,
        mesh=torus,
        in_specs=placed,
        out_specs=(P(leaf, "sep", None, None), P("sep", leaf, None)),
        check_vma=False,
    )
```

```python
import functools

import jax
import jax.numpy as jnp
from jax import lax
from jax.experimental import pallas as pl
from jax.experimental.pallas import tpu as pltpu
from jax.sharding import Mesh, PartitionSpec as P

TILE = 128
SHIFT = 7
DEAD = 255
SLOTS = 8
EXTRA = 8
F32 = jnp.float32
BF16 = jnp.bfloat16

SMEM = functools.partial(pl.BlockSpec, memory_space=pltpu.SMEM)
VMEM = functools.partial(pl.BlockSpec, memory_space=pltpu.VMEM)


def near(value):
    return pltpu.with_memory_space_constraint(value, pltpu.VMEM)


def call(kernel, out_shape, in_specs, scratch=(), out_specs=None):
    single = not isinstance(out_shape, (tuple, list))
    if out_specs is None:
        out_specs = VMEM() if single else tuple(VMEM() for _ in out_shape)
    return pl.pallas_call(
        kernel,
        out_shape=out_shape,
        in_specs=in_specs,
        out_specs=out_specs,
        scratch_shapes=list(scratch),
    )


def exchange(value, axes):
    return lax.all_to_all(value, axes, split_axis=0, concat_axis=0, tiled=True)


def over_rows(left, right):
    return lax.dot_general(left, right, (((0,), (0,)), ((), ())), preferred_element_type=F32)


def over_lanes(left, right):
    return lax.dot_general(left, right, (((1,), (1,)), ((), ())), preferred_element_type=F32)


def forward_kernel(
    cols, rows, targets, count, shots, tiles, own_map,
    forward, sent, taken, slots,
    rounded, exact, picked, filled, *, strip,
):
    count_rows, per_row = tiles.shape[0], tiles.shape[1]
    peers, _, width = sent.shape
    kmax = taken.shape[0]
    rounded[...] = shots[...].astype(BF16)
    for t in range(count_rows):
        total = None
        for k in range(0, per_row, 2):
            left = jnp.concatenate([tiles[t, k], tiles[t, k + 1]], axis=1)
            starts = [pl.multiple_of(cols[k + i, t] * TILE, TILE) for i in range(2)]
            right = jnp.concatenate([rounded[pl.ds(s, TILE), :] for s in starts], axis=0)
            term = jnp.dot(left, right, preferred_element_type=F32)
            total = term if total is None else total + term
        exact[pl.ds(t * TILE, TILE), :] = total
        forward[pl.ds(t * TILE, TILE), :] = total.astype(BF16)
    live = count[0, 0]
    for s in range(filled.shape[0]):
        filled[s] = 0
    lane = lax.broadcasted_iota(jnp.int32, own_map.shape, 1)
    place = jnp.zeros(own_map.shape, jnp.int32)
    most = 0
    for k in range(kmax):
        row = exact[pl.ds(rows[0, k], 1), :]
        taken[pl.ds(k, 1), :] = row
        picked[pl.ds(k, 1), :] = jnp.where(k < live, row, 0.0)
        owner = targets[0, k] // strip
        slot = filled[owner]
        alive = (k < live).astype(jnp.int32)
        filled[owner] = slot + alive
        most = jnp.maximum(most, alive * (slot + 1))
        place = jnp.where(lane == k, slot, place)
        slots[0, k] = jnp.where(k < live, owner * SLOTS + jnp.minimum(slot, SLOTS - 1), -1)
    target = own_map[...]
    high = jnp.where(lane < live, target >> SHIFT, DEAD).astype(F32)
    low = (target & (TILE - 1)).astype(F32)
    picked[pl.ds(kmax, EXTRA), :] = jnp.zeros((EXTRA, width), F32)
    picked[pl.ds(kmax, 1), pl.ds(0, kmax)] = high
    picked[pl.ds(kmax + 1, 1), pl.ds(0, kmax)] = low
    picked[pl.ds(kmax + 2, 1), pl.ds(0, kmax)] = place.astype(F32)
    over = jnp.where(most > SLOTS, 1.0, 0.0)
    picked[pl.ds(kmax + 3, 1), :] = jnp.full((1, width), over, F32)
    whole = picked[...].astype(BF16)
    for p in range(peers):
        sent[p] = whole


def ring_targets(got, n_rows, n_y, strip):
    y = lax.axis_index("y")
    kmax = got.shape[1] - EXTRA
    r = lax.broadcasted_iota(jnp.int32, (n_rows, kmax), 0)
    row_id = ((r // strip) * n_y + y) * strip + r % strip
    row_id = row_id.astype(F32)
    for p in range(got.shape[0]):
        info = got[p, pl.ds(kmax, EXTRA), :].astype(F32)
        target = info[0:1, :kmax] * float(TILE) + info[1:2, :kmax]
        yield p, info, jnp.where(row_id == target, 1.0, 0.0).astype(BF16)


def combine_kernel(got, load, sent, summed, *, n_y, strip):
    peers, _, width = got.shape
    n_z, _, half = sent.shape
    n_rows = n_z * strip
    kmax = got.shape[1] - EXTRA
    total, asked, over = None, None, None
    for p, info, hot in ring_targets(got, n_rows, n_y, strip):
        term = jnp.dot(hot, got[p, pl.ds(0, kmax), :], preferred_element_type=F32)
        total = term if total is None else total + term
        slot = lax.broadcasted_iota(jnp.int32, (TILE, kmax), 0)
        place = info[2:3, :kmax].astype(jnp.int32)
        mine = jnp.where(slot == place + p * SLOTS, 1.0, 0.0)
        mine = jnp.where(place < SLOTS, mine, 0.0).astype(BF16)
        wanted = over_lanes(hot, mine)
        asked = wanted if asked is None else asked + wanted
        flag = info[3:4, :TILE]
        over = flag if over is None else jnp.maximum(over, flag)
    lane = lax.broadcasted_iota(jnp.int32, asked.shape, 1)
    asked = jnp.where(lane < peers * SLOTS, asked, jnp.broadcast_to(over, asked.shape)).astype(BF16)
    summed[...] = -total
    z = lax.axis_index("zh") * 2 + lax.axis_index("zl")
    own = pl.ds(pl.multiple_of(z * strip, strip), strip)
    summed[own, :] = summed[own, :] + load[...]
    halves = [summed[:, pl.ds(h * half, half)].astype(BF16) for h in range(2)]
    for p in range(n_z):
        sent[p, pl.ds(0, n_rows), :] = halves[p % 2]
        sent[p, pl.ds(n_rows, strip), :] = asked[p * strip : (p + 1) * strip]


def residual_kernel(got, sent):
    n_rows = sent.shape[1]
    total = got[0, pl.ds(0, n_rows), :].astype(F32)
    for p in range(1, got.shape[0]):
        total = total + got[p, pl.ds(0, n_rows), :].astype(F32)
    value = total.astype(BF16)
    for p in range(sent.shape[0]):
        sent[p] = value


def separator_kernel(cols, near_cols, strips, near_strips, residual, got, product):
    per_row, sections = cols.shape
    n_y, n_rows, half = residual.shape
    strip = product.shape[1] - EXTRA
    per_tile = TILE // strip
    zl = lax.axis_index("zl")

    def tile(c):
        parts = n_y // per_tile
        y = (c % parts) * per_tile
        at = pl.multiple_of((c // parts) * strip, strip)
        return residual[pl.ds(y, per_tile), pl.ds(at, strip), :].reshape(TILE, half)

    over = got[0, pl.ds(n_rows, EXTRA), :].astype(F32)
    for p in range(1, got.shape[0]):
        over = jnp.maximum(over, got[p, pl.ds(n_rows, EXTRA), :].astype(F32))
    for which, wanted, rows in ((zl, cols, strips), (1 - zl, near_cols, near_strips)):
        for q in range(sections):
            total = None
            for k in range(0, per_row, 2):
                right = jnp.concatenate([tile(wanted[k, q]), tile(wanted[k + 1, q])], axis=0)
                left = rows[q, pl.ds(0, strip), pl.ds(k * TILE, 2 * TILE)]
                term = jnp.dot(left, right, preferred_element_type=F32)
                total = term if total is None else total + term
            product[which * sections + q, pl.ds(0, strip), :] = total
            product[which * sections + q, pl.ds(strip, EXTRA), :] = over


def solution_kernel(got, asked, own, sent, over):
    strip, width = own.shape
    half = got.shape[2]
    sections = got.shape[0] // 2
    most = None
    for h in range(2):
        total = None
        for p in range(h * sections, (h + 1) * sections):
            term = got[p, pl.ds(0, strip), :]
            total = term if total is None else total + term
            flag = got[p, pl.ds(strip, EXTRA), :]
            most = flag if most is None else jnp.maximum(most, flag)
        own[:, pl.ds(h * half, half)] = total
    lane = lax.broadcasted_iota(jnp.int32, most.shape, 1)
    over[0, 0] = (jnp.max(jnp.where(lane == TILE - 1, most, 0.0)) > 0.0).astype(jnp.int32)
    value = own[...].astype(BF16)
    n_z, held, _ = asked.shape
    per = sent.shape[0] // n_z
    for p in range(n_z):
        rows = over_rows(asked[p, pl.ds(held - strip, strip), :], value)[: per * SLOTS]
        sent[pl.ds(p * per, per)] = rows.astype(BF16).reshape(per, SLOTS, width)


def pick_kernel(got, strips, sent, *, n_y, strip):
    n_rows = strips.shape[0]
    for p, _, hot in ring_targets(got, n_rows, n_y, strip):
        sent[p] = over_rows(hot, strips[...]).astype(BF16)


def transposed_kernel(cols, count, forward, tiles, row_lanes, base, reach, same, wide):
    count_rows, per_row = tiles.shape[0], tiles.shape[1]
    leaf_rows, width = forward.shape
    kmax = same.shape[0]
    wide[...] = jnp.zeros_like(wide)
    lanes = row_lanes[...]
    sums = None
    for t in range(count_rows):
        r = lax.broadcasted_iota(jnp.int32, (TILE, TILE), 0) + t * TILE
        hot = jnp.where(r == lanes, 1.0, 0.0).astype(BF16)
        term = over_rows(hot, hot)
        sums = term if sums is None else sums + term
        block = jnp.concatenate([forward[pl.ds(t * TILE, TILE), :], hot], axis=1)
        for k in range(per_row):
            at = pl.ds(pl.multiple_of(cols[k, t] * TILE, TILE), TILE)
            wide[at, :] = wide[at, :] + over_rows(tiles[t, k], block)
    base[...] = wide[:, pl.ds(0, width)]
    reach[...] = wide[:, pl.ds(width, TILE)].astype(BF16)
    same[...] = sums[:kmax]


def finish(needed, count, taken, same, base, reach, out, change):
    kmax = taken.shape[0]
    equal = same[...][:, :kmax]
    k = lax.broadcasted_iota(jnp.int32, equal.shape, 1)
    mine = lax.broadcasted_iota(jnp.int32, equal.shape, 0)
    earlier = jnp.sum(jnp.where(k < mine, equal, 0.0), axis=1, keepdims=True)
    live = jnp.where(k < count[0, 0], equal, 0.0).astype(BF16)
    term = jnp.dot(live, needed().astype(BF16), preferred_element_type=F32)
    before = taken[...]
    delta = (before - term).astype(BF16).astype(F32) - before.astype(BF16).astype(F32)
    delta = jnp.where(earlier == 0.0, delta, 0.0)
    high = delta.astype(BF16)
    change[pl.ds(0, kmax), :] = high
    change[pl.ds(kmax, kmax), :] = (delta - high.astype(F32)).astype(BF16)
    out[...] = base[...] + jnp.dot(reach[...], change[...], preferred_element_type=F32)


def slot_finish_kernel(slots, count, got, taken, same, base, reach, out, change, plain, rows):
    kmax = taken.shape[0]

    def needed():
        plain[...] = got[...].reshape(plain.shape).astype(F32)
        for k in range(kmax):
            at = slots[0, k]
            row = plain[pl.ds(jnp.maximum(at, 0), 1), :]
            rows[pl.ds(k, 1), :] = jnp.where(at >= 0, row, 0.0)
        return rows[...]

    finish(needed, count, taken, same, base, reach, out, change)


def ring_finish_kernel(count, got, taken, same, base, reach, out, change):
    def needed():
        total = got[0].astype(F32)
        for p in range(1, got.shape[0]):
            total = total + got[p].astype(F32)
        return total

    finish(needed, count, taken, same, base, reach, out, change)


def body(
    shot_columns,
    factor_tiles,
    factor_cols,
    boundary_rows,
    boundary_map,
    boundary_count,
    separator_load,
    inverse_tiles,
    inverse_cols,
):
    z_axes = ("zh", "zl")
    n_z, n_y = lax.axis_size(z_axes), lax.axis_size("y")
    n_sep, n_leaf = lax.axis_size("sep"), n_z * n_y
    shots, tiles, cols = shot_columns[0, 0], factor_tiles[0, 0], factor_cols[0, 0].T
    rows, own_map, load = boundary_rows[0], boundary_map[0], separator_load[0]
    leaf_rows, width = shots.shape
    kmax = rows.shape[1]
    strip = load.shape[0]
    shape = jax.ShapeDtypeStruct
    tile_cols = inverse_cols[:, 0, 0]
    strips = inverse_tiles[:, :, 0].reshape(n_sep, strip, -1)
    noted = jnp.pad(
        tile_cols.astype(BF16)[:, None],
        ((0, 0), (0, EXTRA - 1), (0, strips.shape[2] - tile_cols.shape[1])),
    )
    bundle = jnp.concatenate([strips, noted], axis=1)
    near_bundle = lax.ppermute(bundle, "zl", [(0, 1), (1, 0)])
    near_cols = near_bundle[:, strip, : tile_cols.shape[1]].astype(jnp.int32)
    forward, sent, taken, slots = call(
        functools.partial(forward_kernel, strip=strip),
        (
            shape((leaf_rows, width), BF16),
            shape((n_y, kmax + EXTRA, width), BF16),
            shape((kmax, width), F32),
            shape((1, kmax), jnp.int32),
        ),
        [SMEM(), SMEM(), SMEM(), SMEM(), VMEM(), VMEM(), VMEM()],
        [
            pltpu.VMEM((leaf_rows, width), BF16),
            pltpu.VMEM((leaf_rows, width), F32),
            pltpu.VMEM((kmax + EXTRA, width), F32),
            pltpu.SMEM((n_leaf,), jnp.int32),
        ],
        (VMEM(), VMEM(), VMEM(), SMEM()),
    )(cols, rows, own_map, boundary_count, shots, tiles, own_map)
    ring = exchange(sent, "y")
    half = width // 2
    sent = call(
        functools.partial(combine_kernel, n_y=n_y, strip=strip),
        shape((n_z, n_z * strip + strip, half), BF16),
        [VMEM(), VMEM()],
        [pltpu.VMEM((n_z * strip, width), F32)],
    )(near(ring), load)
    asked = exchange(sent, z_axes)
    sent = call(residual_kernel, shape((n_y, n_z * strip, half), BF16), [VMEM()])(near(asked))
    residual = exchange(sent, "y")
    held_rows, _ = lax.optimization_barrier((rows, asked[0, 0, 0]))
    base, reach, same = call(
        transposed_kernel,
        (shape((leaf_rows, width), F32), shape((leaf_rows, TILE), BF16), shape((kmax, TILE), F32)),
        [SMEM(), SMEM(), VMEM(), VMEM(), VMEM()],
        [pltpu.VMEM((leaf_rows, width + TILE), F32)],
    )(cols, boundary_count, forward, tiles, jnp.concatenate([held_rows, held_rows], axis=1))
    product = call(
        separator_kernel,
        shape((2 * n_sep, strip + EXTRA, half), F32),
        [SMEM(), SMEM(), VMEM(), VMEM(), VMEM(), VMEM()],
    )(tile_cols.T, near_cols.T, near(bundle), near(near_bundle), near(residual), near(asked))
    got = exchange(product, ("zl", "sep"))
    own, sent, over = call(
        solution_kernel,
        (shape((strip, width), F32), shape((n_leaf, SLOTS, width), BF16), shape((1, 1), jnp.int32)),
        [VMEM(), VMEM()],
        out_specs=(VMEM(), VMEM(), SMEM()),
    )(near(got), near(asked))

    def finished(kernel, lead, scratch):
        return call(
            kernel,
            shape((leaf_rows, width), F32),
            lead + [VMEM(), VMEM(), VMEM(), VMEM()],
            [pltpu.VMEM((2 * kmax, width), BF16)] + scratch,
        )

    def by_slots():
        got = exchange(sent, z_axes + ("y",))
        return finished(
            slot_finish_kernel,
            [SMEM(), SMEM(), VMEM()],
            [pltpu.VMEM((n_leaf * SLOTS, width), F32), pltpu.VMEM((kmax, width), F32)],
        )(slots, boundary_count, near(got), taken, same, base, reach)

    def by_rings():
        value = jnp.broadcast_to(own.astype(BF16)[None], (n_z, strip, width))
        solved = exchange(value, z_axes).reshape(-1, width)
        picked = call(
            functools.partial(pick_kernel, n_y=n_y, strip=strip),
            shape((n_y, kmax, width), BF16),
            [VMEM(), VMEM()],
        )(ring, solved)
        got = exchange(picked, "y")
        return finished(ring_finish_kernel, [SMEM(), VMEM()], [])(
            boundary_count, near(got), taken, same, base, reach
        )

    leaf_solution = lax.cond(over[0, 0] > 0, by_rings, by_slots)
    return leaf_solution[None, None], own[None]


def solution(mesh):
    n_leaf, n_sep = mesh.shape["leaf"], mesh.shape["sep"]
    n_y = 8
    torus = Mesh(mesh.devices.reshape(n_leaf // n_y // 2, 2, n_y, n_sep), ("zh", "zl", "y", "sep"))
    leaf = ("zh", "zl", "y")
    placed = (
        P(leaf, "sep", None, None),
        P(leaf, "sep", None, None, None, None),
        P(leaf, "sep", None, None),
        P(leaf, "sep", None),
        P(leaf, "sep", None),
        P(leaf, "sep"),
        P("sep", leaf, None),
        P(None, leaf, "sep", None, None),
        P(None, leaf, "sep", None),
    )
    return jax.shard_map(
        body,
        mesh=torus,
        in_specs=placed,
        out_specs=(P(leaf, "sep", None, None), P("sep", leaf, None)),
        check_vma=False,
    )
```

```python
import functools

import jax
import jax.numpy as jnp
from jax import lax
from jax.experimental import pallas as pl
from jax.experimental.pallas import tpu as pltpu
from jax.sharding import Mesh, PartitionSpec as P

TILE = 128
SHIFT = 7
DEAD = 255
SLOTS = 8
EXTRA = 8
PIECES = 4
F32 = jnp.float32
BF16 = jnp.bfloat16

SMEM = functools.partial(pl.BlockSpec, memory_space=pltpu.SMEM)
VMEM = functools.partial(pl.BlockSpec, memory_space=pltpu.VMEM)
ANY = functools.partial(pl.BlockSpec, memory_space=pl.ANY)


def near(value):
    return pltpu.with_memory_space_constraint(value, pltpu.VMEM)


def call(kernel, out_shape, in_specs, scratch=(), out_specs=None):
    single = not isinstance(out_shape, (tuple, list))
    if out_specs is None:
        out_specs = VMEM() if single else tuple(VMEM() for _ in out_shape)
    return pl.pallas_call(
        kernel,
        out_shape=out_shape,
        in_specs=in_specs,
        out_specs=out_specs,
        scratch_shapes=list(scratch),
    )


def exchange(value, axes):
    return lax.all_to_all(value, axes, split_axis=0, concat_axis=0, tiled=True)


def chunks(source, target, sems):
    n = sems.shape[0]
    size = source.shape[0] // n
    made = []
    for i in range(n):
        at = pl.ds(i * size, size)
        made.append((at, pltpu.make_async_copy(source.at[at], target.at[at], sems.at[i])))
    return made


def over_rows(left, right):
    return lax.dot_general(left, right, (((0,), (0,)), ((), ())), preferred_element_type=F32)


def over_lanes(left, right):
    return lax.dot_general(left, right, (((1,), (1,)), ((), ())), preferred_element_type=F32)


def forward_kernel(
    cols, rows, targets, count, far_shots, far_tiles, own_map,
    forward, sent, taken, slots,
    shots, tiles, shot_sems, tile_sems, rounded, exact, picked, filled, *, strip,
):
    count_rows, per_row = tiles.shape[0], tiles.shape[1]
    shot_copies = chunks(far_shots, shots, shot_sems)
    tile_copies = chunks(far_tiles, tiles, tile_sems)
    for _, copy in shot_copies + tile_copies:
        copy.start()
    peers, _, width = sent.shape
    kmax = taken.shape[0]
    live = count[0, 0]
    for s in range(filled.shape[0]):
        filled[s] = 0
    lane = lax.broadcasted_iota(jnp.int32, own_map.shape, 1)
    place = jnp.zeros(own_map.shape, jnp.int32)
    most = 0
    for k in range(kmax):
        owner = targets[0, k] // strip
        slot = filled[owner]
        alive = (k < live).astype(jnp.int32)
        filled[owner] = slot + alive
        most = jnp.maximum(most, alive * (slot + 1))
        place = jnp.where(lane == k, slot, place)
        slots[0, k] = jnp.where(k < live, owner * SLOTS + jnp.minimum(slot, SLOTS - 1), -1)
    for at, copy in shot_copies:
        copy.wait()
        rounded[at] = shots[at].astype(BF16)
    span = count_rows // len(tile_copies)
    for t in range(count_rows):
        if t % span == 0:
            tile_copies[t // span][1].wait()
        total = None
        for k in range(0, per_row, 2):
            left = jnp.concatenate([tiles[t, k], tiles[t, k + 1]], axis=1)
            starts = [pl.multiple_of(cols[k + i, t] * TILE, TILE) for i in range(2)]
            right = jnp.concatenate([rounded[pl.ds(s, TILE), :] for s in starts], axis=0)
            term = jnp.dot(left, right, preferred_element_type=F32)
            total = term if total is None else total + term
        exact[pl.ds(t * TILE, TILE), :] = total
        forward[pl.ds(t * TILE, TILE), :] = total.astype(BF16)
    for k in range(kmax):
        row = exact[pl.ds(rows[0, k], 1), :]
        taken[pl.ds(k, 1), :] = row
        picked[pl.ds(k, 1), :] = jnp.where(k < live, row, 0.0)
    target = own_map[...]
    high = jnp.where(lane < live, target >> SHIFT, DEAD).astype(F32)
    low = (target & (TILE - 1)).astype(F32)
    picked[pl.ds(kmax, EXTRA), :] = jnp.zeros((EXTRA, width), F32)
    picked[pl.ds(kmax, 1), pl.ds(0, kmax)] = high
    picked[pl.ds(kmax + 1, 1), pl.ds(0, kmax)] = low
    picked[pl.ds(kmax + 2, 1), pl.ds(0, kmax)] = place.astype(F32)
    over = jnp.where(most > SLOTS, 1.0, 0.0)
    picked[pl.ds(kmax + 3, 1), :] = jnp.full((1, width), over, F32)
    whole = picked[...].astype(BF16)
    for p in range(peers):
        sent[p] = whole


def ring_targets(got, n_rows, n_y, strip):
    y = lax.axis_index("y")
    kmax = got.shape[1] - EXTRA
    r = lax.broadcasted_iota(jnp.int32, (n_rows, kmax), 0)
    row_id = ((r // strip) * n_y + y) * strip + r % strip
    row_id = row_id.astype(F32)
    for p in range(got.shape[0]):
        info = got[p, pl.ds(kmax, EXTRA), :].astype(F32)
        target = info[0:1, :kmax] * float(TILE) + info[1:2, :kmax]
        yield p, info, jnp.where(row_id == target, 1.0, 0.0).astype(BF16)


def combine_kernel(got, load, sent, summed, *, n_y, strip):
    peers, _, width = got.shape
    n_z, _, half = sent.shape
    n_rows = n_z * strip
    kmax = got.shape[1] - EXTRA
    total, asked, over = None, None, None
    for p, info, hot in ring_targets(got, n_rows, n_y, strip):
        term = jnp.dot(hot, got[p, pl.ds(0, kmax), :], preferred_element_type=F32)
        total = term if total is None else total + term
        slot = lax.broadcasted_iota(jnp.int32, (TILE, kmax), 0)
        place = info[2:3, :kmax].astype(jnp.int32)
        mine = jnp.where(slot == place + p * SLOTS, 1.0, 0.0)
        mine = jnp.where(place < SLOTS, mine, 0.0).astype(BF16)
        wanted = over_lanes(hot, mine)
        asked = wanted if asked is None else asked + wanted
        flag = info[3:4, :TILE]
        over = flag if over is None else jnp.maximum(over, flag)
    lane = lax.broadcasted_iota(jnp.int32, asked.shape, 1)
    asked = jnp.where(lane < peers * SLOTS, asked, jnp.broadcast_to(over, asked.shape)).astype(BF16)
    summed[...] = -total
    z = lax.axis_index("zh") * 2 + lax.axis_index("zl")
    own = pl.ds(pl.multiple_of(z * strip, strip), strip)
    summed[own, :] = summed[own, :] + load[...]
    halves = [summed[:, pl.ds(h * half, half)].astype(BF16) for h in range(2)]
    for p in range(n_z):
        sent[p, pl.ds(0, n_rows), :] = halves[p % 2]
        sent[p, pl.ds(n_rows, strip), :] = asked[p * strip : (p + 1) * strip]


def residual_kernel(got, sent):
    n_rows = sent.shape[1]
    total = got[0, pl.ds(0, n_rows), :].astype(F32)
    for p in range(1, got.shape[0]):
        total = total + got[p, pl.ds(0, n_rows), :].astype(F32)
    value = total.astype(BF16)
    for p in range(sent.shape[0]):
        sent[p] = value


def separator_kernel(cols, near_cols, strips, near_strips, residual, got, product):
    per_row, sections = cols.shape
    n_y, n_rows, half = residual.shape
    strip = product.shape[1] - EXTRA
    per_tile = TILE // strip
    zl = lax.axis_index("zl")

    def tile(c):
        parts = n_y // per_tile
        y = (c % parts) * per_tile
        at = pl.multiple_of((c // parts) * strip, strip)
        return residual[pl.ds(y, per_tile), pl.ds(at, strip), :].reshape(TILE, half)

    over = got[0, pl.ds(n_rows, EXTRA), :].astype(F32)
    for p in range(1, got.shape[0]):
        over = jnp.maximum(over, got[p, pl.ds(n_rows, EXTRA), :].astype(F32))
    for which, wanted, rows in ((zl, cols, strips), (1 - zl, near_cols, near_strips)):
        for q in range(sections):
            total = None
            for k in range(0, per_row, 2):
                right = jnp.concatenate([tile(wanted[k, q]), tile(wanted[k + 1, q])], axis=0)
                left = rows[q, pl.ds(0, strip), pl.ds(k * TILE, 2 * TILE)]
                term = jnp.dot(left, right, preferred_element_type=F32)
                total = term if total is None else total + term
            product[which * sections + q, pl.ds(0, strip), :] = total
            product[which * sections + q, pl.ds(strip, EXTRA), :] = over


def solution_kernel(got, asked, own, sent, over):
    strip, width = own.shape
    half = got.shape[2]
    sections = got.shape[0] // 2
    most = None
    for h in range(2):
        total = None
        for p in range(h * sections, (h + 1) * sections):
            term = got[p, pl.ds(0, strip), :]
            total = term if total is None else total + term
            flag = got[p, pl.ds(strip, EXTRA), :]
            most = flag if most is None else jnp.maximum(most, flag)
        own[:, pl.ds(h * half, half)] = total
    lane = lax.broadcasted_iota(jnp.int32, most.shape, 1)
    over[0, 0] = (jnp.max(jnp.where(lane == TILE - 1, most, 0.0)) > 0.0).astype(jnp.int32)
    value = own[...].astype(BF16)
    n_z, held, _ = asked.shape
    per = sent.shape[0] // n_z
    for p in range(n_z):
        rows = over_rows(asked[p, pl.ds(held - strip, strip), :], value)[: per * SLOTS]
        sent[pl.ds(p * per, per)] = rows.astype(BF16).reshape(per, SLOTS, width)


def pick_kernel(got, strips, sent, *, n_y, strip):
    n_rows = strips.shape[0]
    for p, _, hot in ring_targets(got, n_rows, n_y, strip):
        sent[p] = over_rows(hot, strips[...]).astype(BF16)


def transposed_kernel(cols, count, forward, tiles, row_lanes, base, reach, same, wide):
    count_rows, per_row = tiles.shape[0], tiles.shape[1]
    leaf_rows, width = forward.shape
    kmax = same.shape[0]
    wide[...] = jnp.zeros_like(wide)
    lanes = row_lanes[...]
    sums = None
    for t in range(count_rows):
        r = lax.broadcasted_iota(jnp.int32, (TILE, TILE), 0) + t * TILE
        hot = jnp.where(r == lanes, 1.0, 0.0).astype(BF16)
        term = over_rows(hot, hot)
        sums = term if sums is None else sums + term
        block = jnp.concatenate([forward[pl.ds(t * TILE, TILE), :], hot], axis=1)
        for k in range(per_row):
            at = pl.ds(pl.multiple_of(cols[k, t] * TILE, TILE), TILE)
            wide[at, :] = wide[at, :] + over_rows(tiles[t, k], block)
    base[...] = wide[:, pl.ds(0, width)]
    reach[...] = wide[:, pl.ds(width, TILE)].astype(BF16)
    same[...] = sums[:kmax]


def finish(needed, count, taken, same, base, reach, out, change, held, in_sems, out_sems):
    arrivals = chunks(base, held, in_sems)
    leaves = chunks(held, out, out_sems)
    for _, copy in arrivals:
        copy.start()
    kmax = taken.shape[0]
    equal = same[...][:, :kmax]
    k = lax.broadcasted_iota(jnp.int32, equal.shape, 1)
    mine = lax.broadcasted_iota(jnp.int32, equal.shape, 0)
    earlier = jnp.sum(jnp.where(k < mine, equal, 0.0), axis=1, keepdims=True)
    live = jnp.where(k < count[0, 0], equal, 0.0).astype(BF16)
    term = jnp.dot(live, needed().astype(BF16), preferred_element_type=F32)
    before = taken[...]
    delta = (before - term).astype(BF16).astype(F32) - before.astype(BF16).astype(F32)
    delta = jnp.where(earlier == 0.0, delta, 0.0)
    high = delta.astype(BF16)
    change[pl.ds(0, kmax), :] = high
    change[pl.ds(kmax, kmax), :] = (delta - high.astype(F32)).astype(BF16)
    for (at, arrive), (_, leave) in zip(arrivals, leaves, strict=True):
        arrive.wait()
        held[at] = held[at] + jnp.dot(reach[at], change[...], preferred_element_type=F32)
        leave.start()
    for _, leave in leaves:
        leave.wait()


def slot_finish_kernel(slots, count, got, taken, same, base, reach, out, change, held, in_sems, out_sems, plain, rows):
    kmax = taken.shape[0]

    def needed():
        plain[...] = got[...].reshape(plain.shape).astype(F32)
        for k in range(kmax):
            at = slots[0, k]
            row = plain[pl.ds(jnp.maximum(at, 0), 1), :]
            rows[pl.ds(k, 1), :] = jnp.where(at >= 0, row, 0.0)
        return rows[...]

    finish(needed, count, taken, same, base, reach, out, change, held, in_sems, out_sems)


def ring_finish_kernel(count, got, taken, same, base, reach, out, change, held, in_sems, out_sems):
    def needed():
        total = got[0].astype(F32)
        for p in range(1, got.shape[0]):
            total = total + got[p].astype(F32)
        return total

    finish(needed, count, taken, same, base, reach, out, change, held, in_sems, out_sems)


def body(
    shot_columns,
    factor_tiles,
    factor_cols,
    boundary_rows,
    boundary_map,
    boundary_count,
    separator_load,
    inverse_tiles,
    inverse_cols,
):
    z_axes = ("zh", "zl")
    n_z, n_y = lax.axis_size(z_axes), lax.axis_size("y")
    n_sep, n_leaf = lax.axis_size("sep"), n_z * n_y
    shots, tiles, cols = shot_columns[0, 0], factor_tiles[0, 0], factor_cols[0, 0].T
    rows, own_map, load = boundary_rows[0], boundary_map[0], separator_load[0]
    leaf_rows, width = shots.shape
    kmax = rows.shape[1]
    strip = load.shape[0]
    shape = jax.ShapeDtypeStruct
    tile_cols = inverse_cols[:, 0, 0]
    strips = inverse_tiles[:, :, 0].reshape(n_sep, strip, -1)
    noted = jnp.pad(
        tile_cols.astype(BF16)[:, None],
        ((0, 0), (0, EXTRA - 1), (0, strips.shape[2] - tile_cols.shape[1])),
    )
    bundle = jnp.concatenate([strips, noted], axis=1)
    near_bundle = lax.ppermute(bundle, "zl", [(0, 1), (1, 0)])
    forward, sent, taken, slots = call(
        functools.partial(forward_kernel, strip=strip),
        (
            shape((leaf_rows, width), BF16),
            shape((n_y, kmax + EXTRA, width), BF16),
            shape((kmax, width), F32),
            shape((1, kmax), jnp.int32),
        ),
        [SMEM(), SMEM(), SMEM(), SMEM(), ANY(), ANY(), VMEM()],
        [
            pltpu.VMEM(shots.shape, F32),
            pltpu.VMEM(tiles.shape, BF16),
            pltpu.SemaphoreType.DMA((PIECES,)),
            pltpu.SemaphoreType.DMA((PIECES,)),
            pltpu.VMEM((leaf_rows, width), BF16),
            pltpu.VMEM((leaf_rows, width), F32),
            pltpu.VMEM((kmax + EXTRA, width), F32),
            pltpu.SMEM((n_leaf,), jnp.int32),
        ],
        (VMEM(), VMEM(), VMEM(), SMEM()),
    )(cols, rows, own_map, boundary_count, shots, tiles, own_map)
    ring = exchange(sent, "y")
    ring, near_bundle = lax.optimization_barrier((ring, near_bundle))
    near_cols = near_bundle[:, strip, : tile_cols.shape[1]].astype(jnp.int32)
    half = width // 2
    sent = call(
        functools.partial(combine_kernel, n_y=n_y, strip=strip),
        shape((n_z, n_z * strip + strip, half), BF16),
        [VMEM(), VMEM()],
        [pltpu.VMEM((n_z * strip, width), F32)],
    )(near(ring), load)
    asked = exchange(sent, z_axes)
    sent = call(residual_kernel, shape((n_y, n_z * strip, half), BF16), [VMEM()])(near(asked))
    residual = exchange(sent, "y")
    held_rows, _ = lax.optimization_barrier((rows, asked[0, 0, 0]))
    base, reach, same = call(
        transposed_kernel,
        (shape((leaf_rows, width), F32), shape((leaf_rows, TILE), BF16), shape((kmax, TILE), F32)),
        [SMEM(), SMEM(), VMEM(), VMEM(), VMEM()],
        [pltpu.VMEM((leaf_rows, width + TILE), F32)],
    )(cols, boundary_count, forward, tiles, jnp.concatenate([held_rows, held_rows], axis=1))
    product = call(
        separator_kernel,
        shape((2 * n_sep, strip + EXTRA, half), F32),
        [SMEM(), SMEM(), VMEM(), VMEM(), VMEM(), VMEM()],
    )(tile_cols.T, near_cols.T, near(bundle), near(near_bundle), near(residual), near(asked))
    got = exchange(product, ("zl", "sep"))
    own, sent, over = call(
        solution_kernel,
        (shape((strip, width), F32), shape((n_leaf, SLOTS, width), BF16), shape((1, 1), jnp.int32)),
        [VMEM(), VMEM()],
        out_specs=(VMEM(), VMEM(), SMEM()),
    )(near(got), near(asked))

    def finished(kernel, lead, scratch):
        return call(
            kernel,
            shape((leaf_rows, width), F32),
            lead + [VMEM(), VMEM(), ANY(), VMEM()],
            [
                pltpu.VMEM((2 * kmax, width), BF16),
                pltpu.VMEM((leaf_rows, width), F32),
                pltpu.SemaphoreType.DMA((PIECES,)),
                pltpu.SemaphoreType.DMA((PIECES,)),
            ]
            + scratch,
            ANY(),
        )

    def by_slots():
        got = exchange(sent, z_axes + ("y",))
        return finished(
            slot_finish_kernel,
            [SMEM(), SMEM(), VMEM()],
            [pltpu.VMEM((n_leaf * SLOTS, width), F32), pltpu.VMEM((kmax, width), F32)],
        )(slots, boundary_count, near(got), taken, same, base, reach)

    def by_rings():
        value = jnp.broadcast_to(own.astype(BF16)[None], (n_z, strip, width))
        solved = exchange(value, z_axes).reshape(-1, width)
        picked = call(
            functools.partial(pick_kernel, n_y=n_y, strip=strip),
            shape((n_y, kmax, width), BF16),
            [VMEM(), VMEM()],
        )(ring, solved)
        got = exchange(picked, "y")
        return finished(ring_finish_kernel, [SMEM(), VMEM()], [])(
            boundary_count, near(got), taken, same, base, reach
        )

    leaf_solution = lax.cond(over[0, 0] > 0, by_rings, by_slots)
    return leaf_solution[None, None], own[None]


def solution(mesh):
    n_leaf, n_sep = mesh.shape["leaf"], mesh.shape["sep"]
    n_y = 8
    torus = Mesh(mesh.devices.reshape(n_leaf // n_y // 2, 2, n_y, n_sep), ("zh", "zl", "y", "sep"))
    leaf = ("zh", "zl", "y")
    placed = (
        P(leaf, "sep", None, None),
        P(leaf, "sep", None, None, None, None),
        P(leaf, "sep", None, None),
        P(leaf, "sep", None),
        P(leaf, "sep", None),
        P(leaf, "sep"),
        P("sep", leaf, None),
        P(None, leaf, "sep", None, None),
        P(None, leaf, "sep", None),
    )
    return jax.shard_map(
        body,
        mesh=torus,
        in_specs=placed,
        out_specs=(P(leaf, "sep", None, None), P("sep", leaf, None)),
        check_vma=False,
    )
```

```python
import functools

import jax
import jax.numpy as jnp
from jax import lax
from jax.experimental import pallas as pl
from jax.experimental.pallas import tpu as pltpu
from jax.sharding import Mesh, PartitionSpec as P

TILE = 128
SHIFT = 7
DEAD = 255
SLOTS = 8
EXTRA = 8
F32 = jnp.float32
BF16 = jnp.bfloat16

SMEM = functools.partial(pl.BlockSpec, memory_space=pltpu.SMEM)
VMEM = functools.partial(pl.BlockSpec, memory_space=pltpu.VMEM)


def near(value):
    return pltpu.with_memory_space_constraint(value, pltpu.VMEM)


def call(kernel, out_shape, in_specs, scratch=(), out_specs=None):
    single = not isinstance(out_shape, (tuple, list))
    if out_specs is None:
        out_specs = VMEM() if single else tuple(VMEM() for _ in out_shape)
    return pl.pallas_call(
        kernel,
        out_shape=out_shape,
        in_specs=in_specs,
        out_specs=out_specs,
        scratch_shapes=list(scratch),
    )


def exchange(value, axes):
    return lax.all_to_all(value, axes, split_axis=0, concat_axis=0, tiled=True)


def over_rows(left, right):
    return lax.dot_general(left, right, (((0,), (0,)), ((), ())), preferred_element_type=F32)


def over_lanes(left, right):
    return lax.dot_general(left, right, (((1,), (1,)), ((), ())), preferred_element_type=F32)


def forward_kernel(
    cols, rows, targets, count, shots, tiles, own_map,
    forward, sent, taken, slots,
    rounded, exact, picked, filled, *, strip,
):
    count_rows, per_row = tiles.shape[0], tiles.shape[1]
    peers, _, width = sent.shape
    kmax = taken.shape[0]
    rounded[...] = shots[...].astype(BF16)
    for t in range(count_rows):
        total = None
        for k in range(0, per_row, 2):
            left = jnp.concatenate([tiles[t, k], tiles[t, k + 1]], axis=1)
            starts = [pl.multiple_of(cols[k + i, t] * TILE, TILE) for i in range(2)]
            right = jnp.concatenate([rounded[pl.ds(s, TILE), :] for s in starts], axis=0)
            term = jnp.dot(left, right, preferred_element_type=F32)
            total = term if total is None else total + term
        exact[pl.ds(t * TILE, TILE), :] = total
        forward[pl.ds(t * TILE, TILE), :] = total.astype(BF16)
    live = count[0, 0]
    for s in range(filled.shape[0]):
        filled[s] = 0
    lane = lax.broadcasted_iota(jnp.int32, own_map.shape, 1)
    place = jnp.zeros(own_map.shape, jnp.int32)
    most = 0
    for k in range(kmax):
        row = exact[pl.ds(rows[0, k], 1), :]
        taken[pl.ds(k, 1), :] = row
        picked[pl.ds(k, 1), :] = jnp.where(k < live, row, 0.0)
        owner = targets[0, k] // strip
        slot = filled[owner]
        alive = (k < live).astype(jnp.int32)
        filled[owner] = slot + alive
        most = jnp.maximum(most, alive * (slot + 1))
        place = jnp.where(lane == k, slot, place)
        slots[0, k] = jnp.where(k < live, owner * SLOTS + jnp.minimum(slot, SLOTS - 1), -1)
    target = own_map[...]
    high = jnp.where(lane < live, target >> SHIFT, DEAD).astype(F32)
    low = (target & (TILE - 1)).astype(F32)
    picked[pl.ds(kmax, EXTRA), :] = jnp.zeros((EXTRA, width), F32)
    picked[pl.ds(kmax, 1), pl.ds(0, kmax)] = high
    picked[pl.ds(kmax + 1, 1), pl.ds(0, kmax)] = low
    picked[pl.ds(kmax + 2, 1), pl.ds(0, kmax)] = place.astype(F32)
    over = jnp.where(most > SLOTS, 1.0, 0.0)
    picked[pl.ds(kmax + 3, 1), :] = jnp.full((1, width), over, F32)
    whole = picked[...].astype(BF16)
    for p in range(peers):
        sent[p] = whole


def ring_targets(got, n_rows, n_y, strip):
    y = lax.axis_index("y")
    kmax = got.shape[1] - EXTRA
    r = lax.broadcasted_iota(jnp.int32, (n_rows, kmax), 0)
    row_id = ((r // strip) * n_y + y) * strip + r % strip
    row_id = row_id.astype(F32)
    for p in range(got.shape[0]):
        info = got[p, pl.ds(kmax, EXTRA), :].astype(F32)
        target = info[0:1, :kmax] * float(TILE) + info[1:2, :kmax]
        yield p, info, jnp.where(row_id == target, 1.0, 0.0).astype(BF16)


def combine_kernel(got, load, cols, sent, summed, notes, *, n_y, strip):
    peers, _, width = got.shape
    n_z, _, half = sent.shape
    n_rows = n_z * strip
    kmax = got.shape[1] - EXTRA
    total, asked, over = None, None, None
    for p, info, hot in ring_targets(got, n_rows, n_y, strip):
        term = jnp.dot(hot, got[p, pl.ds(0, kmax), :], preferred_element_type=F32)
        total = term if total is None else total + term
        slot = lax.broadcasted_iota(jnp.int32, (TILE, kmax), 0)
        place = info[2:3, :kmax].astype(jnp.int32)
        mine = jnp.where(slot == place + p * SLOTS, 1.0, 0.0)
        mine = jnp.where(place < SLOTS, mine, 0.0).astype(BF16)
        wanted = over_lanes(hot, mine)
        asked = wanted if asked is None else asked + wanted
        flag = info[3:4, :TILE]
        over = flag if over is None else jnp.maximum(over, flag)
    rank = lax.broadcasted_iota(jnp.int32, (strip, TILE), 0).astype(F32) + 1.0
    lane = lax.broadcasted_iota(jnp.int32, over.shape, 1)
    notes[...] = jnp.zeros_like(notes)
    notes[pl.ds(EXTRA // 2, cols.shape[0]), pl.ds(0, cols.shape[1])] = cols[...].astype(F32)
    summed[...] = -total
    z = lax.axis_index("zh") * 2 + lax.axis_index("zl")
    own = pl.ds(pl.multiple_of(z * strip, strip), strip)
    summed[own, :] = summed[own, :] + load[...]
    halves = [summed[:, pl.ds(h * half, half)].astype(BF16) for h in range(2)]
    for p in range(n_z):
        sent[p, pl.ds(0, n_rows), :] = halves[p % 2]
        row = jnp.sum(asked[p * strip : (p + 1) * strip] * rank, axis=0, keepdims=True)
        notes[pl.ds(0, 1), :] = jnp.where(lane < peers * SLOTS, row, over)
        sent[p, pl.ds(n_rows, EXTRA), :] = notes[...].astype(BF16)


def residual_kernel(got, sent):
    n_rows = sent.shape[1]
    total = got[0, pl.ds(0, n_rows), :].astype(F32)
    for p in range(1, got.shape[0]):
        total = total + got[p, pl.ds(0, n_rows), :].astype(F32)
    value = total.astype(BF16)
    for p in range(sent.shape[0]):
        sent[p] = value


def separator_kernel(cols, near_cols, strips, near_strips, residual, got, product):
    per_row, sections = cols.shape
    n_y, n_rows, half = residual.shape
    strip = product.shape[1] - EXTRA
    per_tile = TILE // strip
    zl = lax.axis_index("zl")

    def tile(c):
        parts = n_y // per_tile
        y = (c % parts) * per_tile
        at = pl.multiple_of((c // parts) * strip, strip)
        return residual[pl.ds(y, per_tile), pl.ds(at, strip), :].reshape(TILE, half)

    over = got[0, pl.ds(n_rows, EXTRA), :].astype(F32)
    for p in range(1, got.shape[0]):
        over = jnp.maximum(over, got[p, pl.ds(n_rows, EXTRA), :].astype(F32))
    for which, wanted, rows in ((zl, cols, strips), (1 - zl, near_cols, near_strips)):
        for q in range(sections):
            total = None
            for k in range(0, per_row, 2):
                right = jnp.concatenate([tile(wanted[k, q]), tile(wanted[k + 1, q])], axis=0)
                left = rows[q, pl.ds(0, strip), pl.ds(k * TILE, 2 * TILE)]
                term = jnp.dot(left, right, preferred_element_type=F32)
                total = term if total is None else total + term
            product[which * sections + q, pl.ds(0, strip), :] = total
            product[which * sections + q, pl.ds(strip, EXTRA), :] = over


def solution_kernel(got, asked, own, sent, over):
    strip, width = own.shape
    half = got.shape[2]
    sections = got.shape[0] // 2
    most = None
    for h in range(2):
        total = None
        for p in range(h * sections, (h + 1) * sections):
            term = got[p, pl.ds(0, strip), :]
            total = term if total is None else total + term
            flag = got[p, pl.ds(strip, EXTRA), :]
            most = flag if most is None else jnp.maximum(most, flag)
        own[:, pl.ds(h * half, half)] = total
    lane = lax.broadcasted_iota(jnp.int32, most.shape, 1)
    over[0, 0] = (jnp.max(jnp.where(lane == TILE - 1, most, 0.0)) > 0.0).astype(jnp.int32)
    value = own[...].astype(BF16)
    n_z, held, _ = asked.shape
    per = sent.shape[0] // n_z
    rank = lax.broadcasted_iota(jnp.int32, (strip, TILE), 0).astype(F32) + 1.0
    for p in range(n_z):
        row = asked[p, pl.ds(held - EXTRA, EXTRA), :].astype(F32)[0:1]
        hot = jnp.where(rank == row, 1.0, 0.0).astype(BF16)
        rows = over_rows(hot, value)[: per * SLOTS]
        sent[pl.ds(p * per, per)] = rows.astype(BF16).reshape(per, SLOTS, width)


def pick_kernel(got, strips, sent, *, n_y, strip):
    n_rows = strips.shape[0]
    for p, _, hot in ring_targets(got, n_rows, n_y, strip):
        sent[p] = over_rows(hot, strips[...]).astype(BF16)


def transposed_kernel(cols, count, forward, tiles, row_lanes, base, reach, same, wide):
    count_rows, per_row = tiles.shape[0], tiles.shape[1]
    leaf_rows, width = forward.shape
    kmax = same.shape[0]
    wide[...] = jnp.zeros_like(wide)
    lanes = row_lanes[...]
    sums = None
    for t in range(count_rows):
        r = lax.broadcasted_iota(jnp.int32, (TILE, TILE), 0) + t * TILE
        hot = jnp.where(r == lanes, 1.0, 0.0).astype(BF16)
        term = over_rows(hot, hot)
        sums = term if sums is None else sums + term
        block = jnp.concatenate([forward[pl.ds(t * TILE, TILE), :], hot], axis=1)
        for k in range(per_row):
            at = pl.ds(pl.multiple_of(cols[k, t] * TILE, TILE), TILE)
            wide[at, :] = wide[at, :] + over_rows(tiles[t, k], block)
    base[...] = wide[:, pl.ds(0, width)]
    reach[...] = wide[:, pl.ds(width, TILE)].astype(BF16)
    same[...] = sums[:kmax]


def finish(needed, count, taken, same, base, reach, out, change):
    kmax = taken.shape[0]
    equal = same[...][:, :kmax]
    k = lax.broadcasted_iota(jnp.int32, equal.shape, 1)
    mine = lax.broadcasted_iota(jnp.int32, equal.shape, 0)
    earlier = jnp.sum(jnp.where(k < mine, equal, 0.0), axis=1, keepdims=True)
    live = jnp.where(k < count[0, 0], equal, 0.0).astype(BF16)
    term = jnp.dot(live, needed().astype(BF16), preferred_element_type=F32)
    before = taken[...]
    delta = (before - term).astype(BF16).astype(F32) - before.astype(BF16).astype(F32)
    delta = jnp.where(earlier == 0.0, delta, 0.0)
    high = delta.astype(BF16)
    change[pl.ds(0, kmax), :] = high
    change[pl.ds(kmax, kmax), :] = (delta - high.astype(F32)).astype(BF16)
    out[...] = base[...] + jnp.dot(reach[...], change[...], preferred_element_type=F32)


def finish_kernel(slots, count, over, got, other, taken, same, base, reach, out, change, plain, rows):
    kmax = taken.shape[0]

    def needed():
        plain[...] = got[...].reshape(plain.shape).astype(F32)
        for k in range(kmax):
            at = slots[0, k]
            row = plain[pl.ds(jnp.maximum(at, 0), 1), :]
            rows[pl.ds(k, 1), :] = jnp.where(at >= 0, row, 0.0)
        return jnp.where(over[0, 0] > 0, other[...].astype(F32), rows[...])

    finish(needed, count, taken, same, base, reach, out, change)


def body(
    shot_columns,
    factor_tiles,
    factor_cols,
    boundary_rows,
    boundary_map,
    boundary_count,
    separator_load,
    inverse_tiles,
    inverse_cols,
):
    z_axes = ("zh", "zl")
    n_z, n_y = lax.axis_size(z_axes), lax.axis_size("y")
    n_sep, n_leaf = lax.axis_size("sep"), n_z * n_y
    shots, tiles, cols = shot_columns[0, 0], factor_tiles[0, 0], factor_cols[0, 0].T
    rows, own_map, load = boundary_rows[0], boundary_map[0], separator_load[0]
    leaf_rows, width = shots.shape
    kmax = rows.shape[1]
    strip = load.shape[0]
    shape = jax.ShapeDtypeStruct
    tile_cols = inverse_cols[:, 0, 0].T
    strips = inverse_tiles[:, :, 0].reshape(n_sep, strip, -1)
    near_strips = lax.ppermute(strips, "zl", [(0, 1), (1, 0)])
    forward, sent, taken, slots = call(
        functools.partial(forward_kernel, strip=strip),
        (
            shape((leaf_rows, width), BF16),
            shape((n_y, kmax + EXTRA, width), BF16),
            shape((kmax, width), F32),
            shape((1, kmax), jnp.int32),
        ),
        [SMEM(), SMEM(), SMEM(), SMEM(), VMEM(), VMEM(), VMEM()],
        [
            pltpu.VMEM((leaf_rows, width), BF16),
            pltpu.VMEM((leaf_rows, width), F32),
            pltpu.VMEM((kmax + EXTRA, width), F32),
            pltpu.SMEM((n_leaf,), jnp.int32),
        ],
        (VMEM(), VMEM(), VMEM(), SMEM()),
    )(cols, rows, own_map, boundary_count, shots, tiles, own_map)
    ring = exchange(sent, "y")
    half = width // 2
    sent = call(
        functools.partial(combine_kernel, n_y=n_y, strip=strip),
        shape((n_z, n_z * strip + EXTRA, half), BF16),
        [VMEM(), VMEM(), VMEM()],
        [pltpu.VMEM((n_z * strip, width), F32), pltpu.VMEM((EXTRA, half), F32)],
    )(near(ring), load, tile_cols)
    asked = exchange(sent, z_axes)
    beside = lax.axis_index("zh") * 2 + 1 - lax.axis_index("zl")
    near_cols = lax.dynamic_slice(
        asked, (beside, n_z * strip + EXTRA // 2, 0), (1,) + tile_cols.shape
    )[0].astype(jnp.int32)
    sent = call(residual_kernel, shape((n_y, n_z * strip, half), BF16), [VMEM()])(near(asked))
    residual = exchange(sent, "y")
    held_rows, _ = lax.optimization_barrier((rows, asked[0, 0, 0]))
    base, reach, same = call(
        transposed_kernel,
        (
            pltpu.VMEM((leaf_rows, width), F32),
            pltpu.VMEM((leaf_rows, TILE), BF16),
            shape((kmax, TILE), F32),
        ),
        [SMEM(), SMEM(), VMEM(), VMEM(), VMEM()],
        [pltpu.VMEM((leaf_rows, width + TILE), F32)],
    )(cols, boundary_count, forward, tiles, jnp.concatenate([held_rows, held_rows], axis=1))
    product = call(
        separator_kernel,
        shape((2 * n_sep, strip + EXTRA, half), F32),
        [SMEM(), SMEM(), VMEM(), VMEM(), VMEM(), VMEM()],
    )(tile_cols, near_cols, near(strips), near(near_strips), near(residual), near(asked))
    got = exchange(product, ("zl", "sep"))
    own, sent, over = call(
        solution_kernel,
        (shape((strip, width), F32), shape((n_leaf, SLOTS, width), BF16), shape((1, 1), jnp.int32)),
        [VMEM(), VMEM()],
        out_specs=(VMEM(), VMEM(), SMEM()),
    )(near(got), near(asked))

    def by_slots():
        return exchange(sent, z_axes + ("y",)), jnp.zeros((kmax, width), BF16)

    def by_rings():
        value = jnp.broadcast_to(own.astype(BF16)[None], (n_z, strip, width))
        solved = exchange(value, z_axes).reshape(-1, width)
        picked = call(
            functools.partial(pick_kernel, n_y=n_y, strip=strip),
            shape((n_y, kmax, width), BF16),
            [VMEM(), VMEM()],
        )(ring, solved)
        got = exchange(picked, "y")
        return jnp.zeros_like(sent), jnp.sum(got.astype(F32), axis=0).astype(BF16)

    got, other = lax.cond(over[0, 0] > 0, by_rings, by_slots)
    leaf_solution = call(
        finish_kernel,
        shape((leaf_rows, width), F32),
        [SMEM()] * 3 + [VMEM()] * 6,
        [
            pltpu.VMEM((2 * kmax, width), BF16),
            pltpu.VMEM((n_leaf * SLOTS, width), F32),
            pltpu.VMEM((kmax, width), F32),
        ],
    )(slots, boundary_count, over, near(got), other, taken, same, near(base), near(reach))
    return leaf_solution[None, None], own[None]


def solution(mesh):
    n_leaf, n_sep = mesh.shape["leaf"], mesh.shape["sep"]
    n_y = 8
    torus = Mesh(mesh.devices.reshape(n_leaf // n_y // 2, 2, n_y, n_sep), ("zh", "zl", "y", "sep"))
    leaf = ("zh", "zl", "y")
    placed = (
        P(leaf, "sep", None, None),
        P(leaf, "sep", None, None, None, None),
        P(leaf, "sep", None, None),
        P(leaf, "sep", None),
        P(leaf, "sep", None),
        P(leaf, "sep"),
        P("sep", leaf, None),
        P(None, leaf, "sep", None, None),
        P(None, leaf, "sep", None),
    )
    return jax.shard_map(
        body,
        mesh=torus,
        in_specs=placed,
        out_specs=(P(leaf, "sep", None, None), P("sep", leaf, None)),
        check_vma=False,
    )
```

```python
import functools

import jax
import jax.numpy as jnp
from jax import lax
from jax.experimental import pallas as pl
from jax.experimental.pallas import tpu as pltpu
from jax.sharding import Mesh, PartitionSpec as P

TILE = 128
SHIFT = 7
DEAD = 255
SLOTS = 8
EXTRA = 8
F32 = jnp.float32
BF16 = jnp.bfloat16

SMEM = functools.partial(pl.BlockSpec, memory_space=pltpu.SMEM)
VMEM = functools.partial(pl.BlockSpec, memory_space=pltpu.VMEM)


def near(value):
    return pltpu.with_memory_space_constraint(value, pltpu.VMEM)


def call(kernel, out_shape, in_specs, scratch=(), out_specs=None):
    single = not isinstance(out_shape, (tuple, list))
    if out_specs is None:
        out_specs = VMEM() if single else tuple(VMEM() for _ in out_shape)
    return pl.pallas_call(
        kernel,
        out_shape=out_shape,
        in_specs=in_specs,
        out_specs=out_specs,
        scratch_shapes=list(scratch),
    )


def exchange(value, axes):
    return lax.all_to_all(value, axes, split_axis=0, concat_axis=0, tiled=True)


def over_rows(left, right):
    return lax.dot_general(left, right, (((0,), (0,)), ((), ())), preferred_element_type=F32)


def over_lanes(left, right):
    return lax.dot_general(left, right, (((1,), (1,)), ((), ())), preferred_element_type=F32)


def forward_kernel(
    cols, rows, targets, count, shots, tiles, own_map,
    forward, sent, taken, slots,
    rounded, exact, picked, filled, *, strip,
):
    count_rows, per_row = tiles.shape[0], tiles.shape[1]
    peers, _, width = sent.shape
    kmax = taken.shape[0]
    rounded[...] = shots[...].astype(BF16)
    for t in range(count_rows):
        total = None
        for k in range(0, per_row, 2):
            left = jnp.concatenate([tiles[t, k], tiles[t, k + 1]], axis=1)
            starts = [pl.multiple_of(cols[k + i, t] * TILE, TILE) for i in range(2)]
            right = jnp.concatenate([rounded[pl.ds(s, TILE), :] for s in starts], axis=0)
            term = jnp.dot(left, right, preferred_element_type=F32)
            total = term if total is None else total + term
        exact[pl.ds(t * TILE, TILE), :] = total
        forward[pl.ds(t * TILE, TILE), :] = total.astype(BF16)
    live = count[0, 0]
    for s in range(filled.shape[0]):
        filled[s] = 0
    lane = lax.broadcasted_iota(jnp.int32, own_map.shape, 1)
    place = jnp.zeros(own_map.shape, jnp.int32)
    most = 0
    for k in range(kmax):
        row = exact[pl.ds(rows[0, k], 1), :]
        taken[pl.ds(k, 1), :] = row
        picked[pl.ds(k, 1), :] = jnp.where(k < live, row, 0.0)
        owner = targets[0, k] // strip
        slot = filled[owner]
        alive = (k < live).astype(jnp.int32)
        filled[owner] = slot + alive
        most = jnp.maximum(most, alive * (slot + 1))
        place = jnp.where(lane == k, slot, place)
    target = own_map[...]
    slots[...] = jnp.where(lane < live, (target // strip) * SLOTS + jnp.minimum(place, SLOTS - 1), -1)
    high = jnp.where(lane < live, target >> SHIFT, DEAD).astype(F32)
    low = (target & (TILE - 1)).astype(F32)
    picked[pl.ds(kmax, EXTRA), :] = jnp.zeros((EXTRA, width), F32)
    picked[pl.ds(kmax, 1), pl.ds(0, kmax)] = high
    picked[pl.ds(kmax + 1, 1), pl.ds(0, kmax)] = low
    picked[pl.ds(kmax + 2, 1), pl.ds(0, kmax)] = place.astype(F32)
    over = jnp.where(most > SLOTS, 1.0, 0.0)
    picked[pl.ds(kmax + 3, 1), :] = jnp.full((1, width), over, F32)
    whole = picked[...].astype(BF16)
    for p in range(peers):
        sent[p] = whole


def ring_targets(got, n_rows, n_y, strip):
    y = lax.axis_index("y")
    kmax = got.shape[1] - EXTRA
    r = lax.broadcasted_iota(jnp.int32, (n_rows, kmax), 0)
    row_id = ((r // strip) * n_y + y) * strip + r % strip
    row_id = row_id.astype(F32)
    for p in range(got.shape[0]):
        info = got[p, pl.ds(kmax, EXTRA), :].astype(F32)
        target = info[0:1, :kmax] * float(TILE) + info[1:2, :kmax]
        yield p, info, jnp.where(row_id == target, 1.0, 0.0).astype(BF16)


def combine_kernel(got, load, cols, sent, summed, notes, *, n_y, strip):
    peers, _, width = got.shape
    n_z, _, half = sent.shape
    n_rows = n_z * strip
    kmax = got.shape[1] - EXTRA
    total, asked, over = None, None, None
    for p, info, hot in ring_targets(got, n_rows, n_y, strip):
        term = jnp.dot(hot, got[p, pl.ds(0, kmax), :], preferred_element_type=F32)
        total = term if total is None else total + term
        slot = lax.broadcasted_iota(jnp.int32, (TILE, kmax), 0)
        place = info[2:3, :kmax].astype(jnp.int32)
        mine = jnp.where(slot == place + p * SLOTS, 1.0, 0.0)
        mine = jnp.where(place < SLOTS, mine, 0.0).astype(BF16)
        wanted = over_lanes(hot, mine)
        asked = wanted if asked is None else asked + wanted
        flag = info[3:4, :TILE]
        over = flag if over is None else jnp.maximum(over, flag)
    rank = lax.broadcasted_iota(jnp.int32, (strip, TILE), 0).astype(F32) + 1.0
    lane = lax.broadcasted_iota(jnp.int32, over.shape, 1)
    notes[...] = jnp.zeros_like(notes)
    notes[pl.ds(EXTRA // 2, cols.shape[0]), pl.ds(0, cols.shape[1])] = cols[...].astype(F32)
    summed[...] = -total
    z = lax.axis_index("zh") * 2 + lax.axis_index("zl")
    own = pl.ds(pl.multiple_of(z * strip, strip), strip)
    summed[own, :] = summed[own, :] + load[...]
    halves = [summed[:, pl.ds(h * half, half)].astype(BF16) for h in range(2)]
    for p in range(n_z):
        sent[p, pl.ds(0, n_rows), :] = halves[p % 2]
        row = jnp.sum(asked[p * strip : (p + 1) * strip] * rank, axis=0, keepdims=True)
        notes[pl.ds(0, 1), :] = jnp.where(lane < peers * SLOTS, row, over)
        sent[p, pl.ds(n_rows, EXTRA), :] = notes[...].astype(BF16)


def residual_kernel(got, sent):
    n_rows = sent.shape[1]
    total = got[0, pl.ds(0, n_rows), :].astype(F32)
    for p in range(1, got.shape[0]):
        total = total + got[p, pl.ds(0, n_rows), :].astype(F32)
    value = total.astype(BF16)
    for p in range(sent.shape[0]):
        sent[p] = value


def separator_kernel(cols, near_cols, strips, near_strips, residual, got, product):
    per_row, sections = cols.shape
    n_y, n_rows, half = residual.shape
    strip = product.shape[1] - EXTRA
    per_tile = TILE // strip
    zl = lax.axis_index("zl")

    def tile(c):
        parts = n_y // per_tile
        y = (c % parts) * per_tile
        at = pl.multiple_of((c // parts) * strip, strip)
        return residual[pl.ds(y, per_tile), pl.ds(at, strip), :].reshape(TILE, half)

    over = got[0, pl.ds(n_rows, EXTRA), :].astype(F32)
    for p in range(1, got.shape[0]):
        over = jnp.maximum(over, got[p, pl.ds(n_rows, EXTRA), :].astype(F32))
    for which, wanted, rows in ((zl, cols, strips), (1 - zl, near_cols, near_strips)):
        for q in range(sections):
            total = None
            for k in range(0, per_row, 2):
                right = jnp.concatenate([tile(wanted[k, q]), tile(wanted[k + 1, q])], axis=0)
                left = rows[q, pl.ds(0, strip), pl.ds(k * TILE, 2 * TILE)]
                term = jnp.dot(left, right, preferred_element_type=F32)
                total = term if total is None else total + term
            product[which * sections + q, pl.ds(0, strip), :] = total
            product[which * sections + q, pl.ds(strip, EXTRA), :] = over


def solution_kernel(got, asked, own, sent, over):
    strip, width = own.shape
    half = got.shape[2]
    sections = got.shape[0] // 2
    most = None
    for h in range(2):
        total = None
        for p in range(h * sections, (h + 1) * sections):
            term = got[p, pl.ds(0, strip), :]
            total = term if total is None else total + term
            flag = got[p, pl.ds(strip, EXTRA), :]
            most = flag if most is None else jnp.maximum(most, flag)
        own[:, pl.ds(h * half, half)] = total
    lane = lax.broadcasted_iota(jnp.int32, most.shape, 1)
    over[0, 0] = (jnp.max(jnp.where(lane == TILE - 1, most, 0.0)) > 0.0).astype(jnp.int32)
    value = own[...].astype(BF16)
    n_z, held, _ = asked.shape
    per = sent.shape[0] // n_z
    rank = lax.broadcasted_iota(jnp.int32, (strip, TILE), 0).astype(F32) + 1.0
    for p in range(n_z):
        row = asked[p, pl.ds(held - EXTRA, EXTRA), :].astype(F32)[0:1]
        hot = jnp.where(rank == row, 1.0, 0.0).astype(BF16)
        rows = over_rows(hot, value)[: per * SLOTS]
        sent[pl.ds(p * per, per)] = rows.astype(BF16).reshape(per, SLOTS, width)


def pick_kernel(got, strips, sent, *, n_y, strip):
    n_rows = strips.shape[0]
    for p, _, hot in ring_targets(got, n_rows, n_y, strip):
        sent[p] = over_rows(hot, strips[...]).astype(BF16)


def transposed_kernel(cols, count, forward, tiles, row_lanes, base, reach, same, wide):
    count_rows, per_row = tiles.shape[0], tiles.shape[1]
    leaf_rows, width = forward.shape
    kmax = same.shape[0]
    wide[...] = jnp.zeros_like(wide)
    lanes = row_lanes[...]
    sums = None
    for t in range(count_rows):
        r = lax.broadcasted_iota(jnp.int32, (TILE, TILE), 0) + t * TILE
        hot = jnp.where(r == lanes, 1.0, 0.0).astype(BF16)
        term = over_rows(hot, hot)
        sums = term if sums is None else sums + term
        block = jnp.concatenate([forward[pl.ds(t * TILE, TILE), :], hot], axis=1)
        for k in range(per_row):
            at = pl.ds(pl.multiple_of(cols[k, t] * TILE, TILE), TILE)
            wide[at, :] = wide[at, :] + over_rows(tiles[t, k], block)
    base[...] = wide[:, pl.ds(0, width)]
    reach[...] = wide[:, pl.ds(width, TILE)].astype(BF16)
    same[...] = sums[:kmax]


def finish(needed, count, taken, same, base, reach, out, change):
    kmax = taken.shape[0]
    equal = same[...][:, :kmax]
    k = lax.broadcasted_iota(jnp.int32, equal.shape, 1)
    mine = lax.broadcasted_iota(jnp.int32, equal.shape, 0)
    earlier = jnp.sum(jnp.where(k < mine, equal, 0.0), axis=1, keepdims=True)
    live = jnp.where(k < count[0, 0], equal, 0.0).astype(BF16)
    term = jnp.dot(live, needed().astype(BF16), preferred_element_type=F32)
    before = taken[...]
    delta = (before - term).astype(BF16).astype(F32) - before.astype(BF16).astype(F32)
    delta = jnp.where(earlier == 0.0, delta, 0.0)
    high = delta.astype(BF16)
    change[pl.ds(0, kmax), :] = high
    change[pl.ds(kmax, kmax), :] = (delta - high.astype(F32)).astype(BF16)
    out[...] = base[...] + jnp.dot(reach[...], change[...], preferred_element_type=F32)


def finish_kernel(count, over, slots, got, other, taken, same, base, reach, out, change):
    def needed():
        n_leaf, per, width = got.shape
        rows = got[...].reshape(n_leaf * per, width)
        at = lax.broadcasted_iota(jnp.int32, (n_leaf * per, slots.shape[1]), 0)
        hot = jnp.where(at == slots[...], 1.0, 0.0).astype(BF16)
        return jnp.where(over[0, 0] > 0, other[...].astype(F32), over_rows(hot, rows))

    finish(needed, count, taken, same, base, reach, out, change)


def body(
    shot_columns,
    factor_tiles,
    factor_cols,
    boundary_rows,
    boundary_map,
    boundary_count,
    separator_load,
    inverse_tiles,
    inverse_cols,
):
    z_axes = ("zh", "zl")
    n_z, n_y = lax.axis_size(z_axes), lax.axis_size("y")
    n_sep, n_leaf = lax.axis_size("sep"), n_z * n_y
    shots, tiles, cols = shot_columns[0, 0], factor_tiles[0, 0], factor_cols[0, 0].T
    rows, own_map, load = boundary_rows[0], boundary_map[0], separator_load[0]
    leaf_rows, width = shots.shape
    kmax = rows.shape[1]
    strip = load.shape[0]
    shape = jax.ShapeDtypeStruct
    tile_cols = inverse_cols[:, 0, 0].T
    strips = inverse_tiles[:, :, 0].reshape(n_sep, strip, -1)
    near_strips = lax.ppermute(strips, "zl", [(0, 1), (1, 0)])
    forward, sent, taken, slots = call(
        functools.partial(forward_kernel, strip=strip),
        (
            shape((leaf_rows, width), BF16),
            shape((n_y, kmax + EXTRA, width), BF16),
            shape((kmax, width), F32),
            shape((1, kmax), jnp.int32),
        ),
        [SMEM(), SMEM(), SMEM(), SMEM(), VMEM(), VMEM(), VMEM()],
        [
            pltpu.VMEM((leaf_rows, width), BF16),
            pltpu.VMEM((leaf_rows, width), F32),
            pltpu.VMEM((kmax + EXTRA, width), F32),
            pltpu.SMEM((n_leaf,), jnp.int32),
        ],
    )(cols, rows, own_map, boundary_count, shots, tiles, own_map)
    ring = exchange(sent, "y")
    half = width // 2
    sent = call(
        functools.partial(combine_kernel, n_y=n_y, strip=strip),
        shape((n_z, n_z * strip + EXTRA, half), BF16),
        [VMEM(), VMEM(), VMEM()],
        [pltpu.VMEM((n_z * strip, width), F32), pltpu.VMEM((EXTRA, half), F32)],
    )(near(ring), near(load), near(tile_cols))
    asked = exchange(sent, z_axes)
    beside = lax.axis_index("zh") * 2 + 1 - lax.axis_index("zl")
    near_cols = lax.dynamic_slice(
        asked, (beside, n_z * strip + EXTRA // 2, 0), (1,) + tile_cols.shape
    )[0].astype(jnp.int32)
    sent = call(residual_kernel, shape((n_y, n_z * strip, half), BF16), [VMEM()])(near(asked))
    residual = exchange(sent, "y")
    held_rows, _ = lax.optimization_barrier((rows, asked[0, 0, 0]))
    base, reach, same = call(
        transposed_kernel,
        (
            pltpu.VMEM((leaf_rows, width), F32),
            pltpu.VMEM((leaf_rows, TILE), BF16),
            shape((kmax, TILE), F32),
        ),
        [SMEM(), SMEM(), VMEM(), VMEM(), VMEM()],
        [pltpu.VMEM((leaf_rows, width + TILE), F32)],
    )(cols, boundary_count, forward, tiles, jnp.concatenate([held_rows, held_rows], axis=1))
    product = call(
        separator_kernel,
        shape((2 * n_sep, strip + EXTRA, half), F32),
        [SMEM(), SMEM(), VMEM(), VMEM(), VMEM(), VMEM()],
    )(tile_cols, near_cols, near(strips), near(near_strips), near(residual), near(asked))
    got = exchange(product, ("zl", "sep"))
    own, sent, over = call(
        solution_kernel,
        (shape((strip, width), F32), shape((n_leaf, SLOTS, width), BF16), shape((1, 1), jnp.int32)),
        [VMEM(), VMEM()],
        out_specs=(VMEM(), VMEM(), SMEM()),
    )(near(got), near(asked))

    def by_slots():
        return exchange(sent, z_axes + ("y",)), jnp.zeros((kmax, width), BF16)

    def by_rings():
        value = jnp.broadcast_to(own.astype(BF16)[None], (n_z, strip, width))
        solved = exchange(value, z_axes).reshape(-1, width)
        picked = call(
            functools.partial(pick_kernel, n_y=n_y, strip=strip),
            shape((n_y, kmax, width), BF16),
            [VMEM(), VMEM()],
        )(ring, solved)
        got = exchange(picked, "y")
        return jnp.zeros_like(sent), jnp.sum(got.astype(F32), axis=0).astype(BF16)

    got, other = lax.cond(over[0, 0] > 0, by_rings, by_slots)
    leaf_solution = call(
        finish_kernel,
        shape((leaf_rows, width), F32),
        [SMEM()] * 2 + [VMEM()] * 7,
        [pltpu.VMEM((2 * kmax, width), BF16)],
    )(
        boundary_count,
        over,
        near(slots),
        near(got),
        near(other),
        near(taken),
        near(same),
        near(base),
        near(reach),
    )
    return leaf_solution[None, None], own[None]


def solution(mesh):
    n_leaf, n_sep = mesh.shape["leaf"], mesh.shape["sep"]
    n_y = 8
    torus = Mesh(mesh.devices.reshape(n_leaf // n_y // 2, 2, n_y, n_sep), ("zh", "zl", "y", "sep"))
    leaf = ("zh", "zl", "y")
    placed = (
        P(leaf, "sep", None, None),
        P(leaf, "sep", None, None, None, None),
        P(leaf, "sep", None, None),
        P(leaf, "sep", None),
        P(leaf, "sep", None),
        P(leaf, "sep"),
        P("sep", leaf, None),
        P(None, leaf, "sep", None, None),
        P(None, leaf, "sep", None),
    )
    return jax.shard_map(
        body,
        mesh=torus,
        in_specs=placed,
        out_specs=(P(leaf, "sep", None, None), P("sep", leaf, None)),
        check_vma=False,
    )
```

```python
import functools

import jax
import jax.numpy as jnp
from jax import lax
from jax.experimental import pallas as pl
from jax.experimental.pallas import tpu as pltpu
from jax.sharding import Mesh, PartitionSpec as P

TILE = 128
SHIFT = 7
DEAD = 255
SLOTS = 8
EXTRA = 8
F32 = jnp.float32
BF16 = jnp.bfloat16

SMEM = functools.partial(pl.BlockSpec, memory_space=pltpu.SMEM)
VMEM = functools.partial(pl.BlockSpec, memory_space=pltpu.VMEM)


def near(value):
    return pltpu.with_memory_space_constraint(value, pltpu.VMEM)


def call(kernel, out_shape, in_specs, scratch=(), out_specs=None):
    single = not isinstance(out_shape, (tuple, list))
    if out_specs is None:
        out_specs = VMEM() if single else tuple(VMEM() for _ in out_shape)
    return pl.pallas_call(
        kernel,
        out_shape=out_shape,
        in_specs=in_specs,
        out_specs=out_specs,
        scratch_shapes=list(scratch),
    )


def exchange(value, axes):
    return lax.all_to_all(value, axes, split_axis=0, concat_axis=0, tiled=True)


def over_rows(left, right):
    return lax.dot_general(left, right, (((0,), (0,)), ((), ())), preferred_element_type=F32)


def over_lanes(left, right):
    return lax.dot_general(left, right, (((1,), (1,)), ((), ())), preferred_element_type=F32)


def forward_kernel(
    cols, rows, targets, count, shots, tiles, own_map,
    forward, sent, taken, slots,
    rounded, exact, picked, filled, *, strip,
):
    count_rows, per_row = tiles.shape[0], tiles.shape[1]
    peers, _, width = sent.shape
    kmax = taken.shape[0]
    rounded[...] = shots[...].astype(BF16)
    for t in range(count_rows):
        total = None
        for k in range(0, per_row, 2):
            left = jnp.concatenate([tiles[t, k], tiles[t, k + 1]], axis=1)
            starts = [pl.multiple_of(cols[k + i, t] * TILE, TILE) for i in range(2)]
            right = jnp.concatenate([rounded[pl.ds(s, TILE), :] for s in starts], axis=0)
            term = jnp.dot(left, right, preferred_element_type=F32)
            total = term if total is None else total + term
        exact[pl.ds(t * TILE, TILE), :] = total
        forward[pl.ds(t * TILE, TILE), :] = total.astype(BF16)
    live = count[0, 0]
    for s in range(filled.shape[0]):
        filled[s] = 0
    lane = lax.broadcasted_iota(jnp.int32, own_map.shape, 1)
    place = jnp.zeros(own_map.shape, jnp.int32)
    most = 0
    for k in range(kmax):
        row = exact[pl.ds(rows[0, k], 1), :]
        taken[pl.ds(k, 1), :] = row
        picked[pl.ds(k, 1), :] = jnp.where(k < live, row, 0.0)
        owner = targets[0, k] // strip
        slot = filled[owner]
        alive = (k < live).astype(jnp.int32)
        filled[owner] = slot + alive
        most = jnp.maximum(most, alive * (slot + 1))
        place = jnp.where(lane == k, slot, place)
    target = own_map[...]
    slots[...] = jnp.where(lane < live, (target // strip) * SLOTS + jnp.minimum(place, SLOTS - 1), -1)
    high = jnp.where(lane < live, target >> SHIFT, DEAD).astype(F32)
    low = (target & (TILE - 1)).astype(F32)
    picked[pl.ds(kmax, EXTRA), :] = jnp.zeros((EXTRA, width), F32)
    picked[pl.ds(kmax, 1), pl.ds(0, kmax)] = high
    picked[pl.ds(kmax + 1, 1), pl.ds(0, kmax)] = low
    picked[pl.ds(kmax + 2, 1), pl.ds(0, kmax)] = place.astype(F32)
    over = jnp.where(most > SLOTS, 1.0, 0.0)
    picked[pl.ds(kmax + 3, 1), :] = jnp.full((1, width), over, F32)
    whole = picked[...].astype(BF16)
    for p in range(peers):
        sent[p] = whole


def ring_targets(got, n_rows, n_y, strip):
    y = lax.axis_index("y")
    kmax = got.shape[1] - EXTRA
    r = lax.broadcasted_iota(jnp.int32, (n_rows, kmax), 0)
    row_id = ((r // strip) * n_y + y) * strip + r % strip
    row_id = row_id.astype(F32)
    for p in range(got.shape[0]):
        info = got[p, pl.ds(kmax, EXTRA), :].astype(F32)
        target = info[0:1, :kmax] * float(TILE) + info[1:2, :kmax]
        yield p, info, jnp.where(row_id == target, 1.0, 0.0).astype(BF16)


def combine_kernel(got, load, cols, sent, summed, notes, *, n_y, strip):
    peers, _, width = got.shape
    n_z, _, half = sent.shape
    n_rows = n_z * strip
    kmax = got.shape[1] - EXTRA
    total, asked, over = None, None, None
    for p, info, hot in ring_targets(got, n_rows, n_y, strip):
        term = jnp.dot(hot, got[p, pl.ds(0, kmax), :], preferred_element_type=F32)
        total = term if total is None else total + term
        slot = lax.broadcasted_iota(jnp.int32, (TILE, kmax), 0)
        place = info[2:3, :kmax].astype(jnp.int32)
        mine = jnp.where(slot == place + p * SLOTS, 1.0, 0.0)
        mine = jnp.where(place < SLOTS, mine, 0.0).astype(BF16)
        wanted = over_lanes(hot, mine)
        asked = wanted if asked is None else asked + wanted
        flag = info[3:4, :TILE]
        over = flag if over is None else jnp.maximum(over, flag)
    rank = lax.broadcasted_iota(jnp.int32, (strip, TILE), 0).astype(F32) + 1.0
    lane = lax.broadcasted_iota(jnp.int32, over.shape, 1)
    notes[...] = jnp.zeros_like(notes)
    notes[pl.ds(EXTRA // 2, cols.shape[0]), pl.ds(0, cols.shape[1])] = cols[...].astype(F32)
    summed[...] = -total
    z = lax.axis_index("zh") * 2 + lax.axis_index("zl")
    own = pl.ds(pl.multiple_of(z * strip, strip), strip)
    summed[own, :] = summed[own, :] + load[...]
    halves = [summed[:, pl.ds(h * half, half)].astype(BF16) for h in range(2)]
    for p in range(n_z):
        sent[p, pl.ds(0, n_rows), :] = halves[p % 2]
        row = jnp.sum(asked[p * strip : (p + 1) * strip] * rank, axis=0, keepdims=True)
        notes[pl.ds(0, 1), :] = jnp.where(lane < peers * SLOTS, row, over)
        sent[p, pl.ds(n_rows, EXTRA), :] = notes[...].astype(BF16)


def residual_kernel(got, sent):
    n_rows = sent.shape[1]
    total = got[0, pl.ds(0, n_rows), :].astype(F32)
    for p in range(1, got.shape[0]):
        total = total + got[p, pl.ds(0, n_rows), :].astype(F32)
    value = total.astype(BF16)
    for p in range(sent.shape[0]):
        sent[p] = value


def separator_kernel(cols, near_cols, strips, near_strips, residual, got, product):
    per_row, sections = cols.shape
    n_y, n_rows, half = residual.shape
    strip = product.shape[1] - EXTRA
    per_tile = TILE // strip
    zl = lax.axis_index("zl")

    own_cols, other_cols = cols[...], near_cols[...]

    def tile(c):
        parts = n_y // per_tile
        y = (c % parts) * per_tile
        at = pl.multiple_of((c // parts) * strip, strip)
        return residual[pl.ds(y, per_tile), pl.ds(at, strip), :].reshape(TILE, half)

    over = got[0, pl.ds(n_rows, EXTRA), :].astype(F32)
    for p in range(1, got.shape[0]):
        over = jnp.maximum(over, got[p, pl.ds(n_rows, EXTRA), :].astype(F32))
    for which, wanted, rows in ((zl, own_cols, strips), (1 - zl, other_cols, near_strips)):
        for q in range(sections):
            total = None
            for k in range(0, per_row, 2):
                right = jnp.concatenate([tile(wanted[k, q]), tile(wanted[k + 1, q])], axis=0)
                left = rows[q, pl.ds(0, strip), pl.ds(k * TILE, 2 * TILE)]
                term = jnp.dot(left, right, preferred_element_type=F32)
                total = term if total is None else total + term
            product[which * sections + q, pl.ds(0, strip), :] = total
            product[which * sections + q, pl.ds(strip, EXTRA), :] = over


def solution_kernel(got, asked, own, sent, over):
    strip, width = own.shape
    half = got.shape[2]
    sections = got.shape[0] // 2
    most = None
    for h in range(2):
        total = None
        for p in range(h * sections, (h + 1) * sections):
            term = got[p, pl.ds(0, strip), :]
            total = term if total is None else total + term
            flag = got[p, pl.ds(strip, EXTRA), :]
            most = flag if most is None else jnp.maximum(most, flag)
        own[:, pl.ds(h * half, half)] = total
    lane = lax.broadcasted_iota(jnp.int32, most.shape, 1)
    over[0, 0] = (jnp.max(jnp.where(lane == TILE - 1, most, 0.0)) > 0.0).astype(jnp.int32)
    value = own[...].astype(BF16)
    n_z, held, _ = asked.shape
    per = sent.shape[0] // n_z
    rank = lax.broadcasted_iota(jnp.int32, (strip, TILE), 0).astype(F32) + 1.0
    for p in range(n_z):
        row = asked[p, pl.ds(held - EXTRA, EXTRA), :].astype(F32)[0:1]
        hot = jnp.where(rank == row, 1.0, 0.0).astype(BF16)
        rows = over_rows(hot, value)[: per * SLOTS]
        sent[pl.ds(p * per, per)] = rows.astype(BF16).reshape(per, SLOTS, width)


def pick_kernel(got, strips, sent, *, n_y, strip):
    n_rows = strips.shape[0]
    for p, _, hot in ring_targets(got, n_rows, n_y, strip):
        sent[p] = over_rows(hot, strips[...]).astype(BF16)


def transposed_kernel(cols, count, forward, tiles, row_lanes, base, reach, same, wide):
    count_rows, per_row = tiles.shape[0], tiles.shape[1]
    leaf_rows, width = forward.shape
    kmax = same.shape[0]
    wide[...] = jnp.zeros_like(wide)
    lanes = row_lanes[...]
    sums = None
    for t in range(count_rows):
        r = lax.broadcasted_iota(jnp.int32, (TILE, TILE), 0) + t * TILE
        hot = jnp.where(r == lanes, 1.0, 0.0).astype(BF16)
        term = over_rows(hot, hot)
        sums = term if sums is None else sums + term
        block = jnp.concatenate([forward[pl.ds(t * TILE, TILE), :], hot], axis=1)
        for k in range(per_row):
            at = pl.ds(pl.multiple_of(cols[k, t] * TILE, TILE), TILE)
            wide[at, :] = wide[at, :] + over_rows(tiles[t, k], block)
    base[...] = wide[:, pl.ds(0, width)]
    reach[...] = wide[:, pl.ds(width, TILE)].astype(BF16)
    same[...] = sums[:kmax]


def finish(needed, count, taken, same, base, reach, out, change):
    kmax = taken.shape[0]
    equal = same[...][:, :kmax]
    k = lax.broadcasted_iota(jnp.int32, equal.shape, 1)
    mine = lax.broadcasted_iota(jnp.int32, equal.shape, 0)
    earlier = jnp.sum(jnp.where(k < mine, equal, 0.0), axis=1, keepdims=True)
    live = jnp.where(k < count[0, 0], equal, 0.0).astype(BF16)
    term = jnp.dot(live, needed().astype(BF16), preferred_element_type=F32)
    before = taken[...]
    delta = (before - term).astype(BF16).astype(F32) - before.astype(BF16).astype(F32)
    delta = jnp.where(earlier == 0.0, delta, 0.0)
    high = delta.astype(BF16)
    change[pl.ds(0, kmax), :] = high
    change[pl.ds(kmax, kmax), :] = (delta - high.astype(F32)).astype(BF16)
    out[...] = base[...] + jnp.dot(reach[...], change[...], preferred_element_type=F32)


def finish_kernel(count, over, slots, got, other, taken, same, base, reach, out, change):
    def needed():
        n_leaf, per, width = got.shape
        rows = got[...].reshape(n_leaf * per, width)
        at = lax.broadcasted_iota(jnp.int32, (n_leaf * per, slots.shape[1]), 0)
        hot = jnp.where(at == slots[...], 1.0, 0.0).astype(BF16)
        return jnp.where(over[0, 0] > 0, other[...].astype(F32), over_rows(hot, rows))

    finish(needed, count, taken, same, base, reach, out, change)


def body(
    shot_columns,
    factor_tiles,
    factor_cols,
    boundary_rows,
    boundary_map,
    boundary_count,
    separator_load,
    inverse_tiles,
    inverse_cols,
):
    z_axes = ("zh", "zl")
    n_z, n_y = lax.axis_size(z_axes), lax.axis_size("y")
    n_sep, n_leaf = lax.axis_size("sep"), n_z * n_y
    shots, tiles, cols = shot_columns[0, 0], factor_tiles[0, 0], factor_cols[0, 0].T
    rows, own_map, load = boundary_rows[0], boundary_map[0], separator_load[0]
    leaf_rows, width = shots.shape
    kmax = rows.shape[1]
    strip = load.shape[0]
    shape = jax.ShapeDtypeStruct
    tile_cols = inverse_cols[:, 0, 0].T
    strips = inverse_tiles[:, :, 0].reshape(n_sep, strip, -1)
    near_strips = lax.ppermute(strips, "zl", [(0, 1), (1, 0)])
    forward, sent, taken, slots = call(
        functools.partial(forward_kernel, strip=strip),
        (
            shape((leaf_rows, width), BF16),
            shape((n_y, kmax + EXTRA, width), BF16),
            shape((kmax, width), F32),
            shape((1, kmax), jnp.int32),
        ),
        [SMEM(), SMEM(), SMEM(), SMEM(), VMEM(), VMEM(), VMEM()],
        [
            pltpu.VMEM((leaf_rows, width), BF16),
            pltpu.VMEM((leaf_rows, width), F32),
            pltpu.VMEM((kmax + EXTRA, width), F32),
            pltpu.SMEM((n_leaf,), jnp.int32),
        ],
    )(cols, rows, own_map, boundary_count, shots, tiles, own_map)
    ring = exchange(sent, "y")
    half = width // 2
    sent = call(
        functools.partial(combine_kernel, n_y=n_y, strip=strip),
        shape((n_z, n_z * strip + EXTRA, half), BF16),
        [VMEM(), VMEM(), VMEM()],
        [pltpu.VMEM((n_z * strip, width), F32), pltpu.VMEM((EXTRA, half), F32)],
    )(near(ring), near(load), near(tile_cols))
    asked = exchange(sent, z_axes)
    held_rows, _ = lax.optimization_barrier((rows, ring[0, 0, :TILE]))
    base, reach, same = call(
        transposed_kernel,
        (
            pltpu.VMEM((leaf_rows, width), F32),
            pltpu.VMEM((leaf_rows, TILE), BF16),
            shape((kmax, TILE), F32),
        ),
        [SMEM(), SMEM(), VMEM(), VMEM(), VMEM()],
        [pltpu.VMEM((leaf_rows, width + TILE), F32)],
    )(cols, boundary_count, forward, tiles, jnp.concatenate([held_rows, held_rows], axis=1))
    asked, same = lax.optimization_barrier((asked, same))
    beside = lax.axis_index("zh") * 2 + 1 - lax.axis_index("zl")
    near_cols = lax.dynamic_slice(
        asked, (beside, n_z * strip + EXTRA // 2, 0), (1,) + tile_cols.shape
    )[0].astype(jnp.int32)
    sent = call(residual_kernel, shape((n_y, n_z * strip, half), BF16), [VMEM()])(near(asked))
    residual = exchange(sent, "y")
    product = call(
        separator_kernel,
        shape((2 * n_sep, strip + EXTRA, half), F32),
        [VMEM()] * 6,
    )(near(tile_cols), near(near_cols), near(strips), near(near_strips), near(residual), near(asked))
    got = exchange(product, ("zl", "sep"))
    own, sent, over = call(
        solution_kernel,
        (shape((strip, width), F32), shape((n_leaf, SLOTS, width), BF16), shape((1, 1), jnp.int32)),
        [VMEM(), VMEM()],
        out_specs=(VMEM(), VMEM(), SMEM()),
    )(near(got), near(asked))

    def by_slots():
        return exchange(sent, z_axes + ("y",)), jnp.zeros((kmax, width), BF16)

    def by_rings():
        value = jnp.broadcast_to(own.astype(BF16)[None], (n_z, strip, width))
        solved = exchange(value, z_axes).reshape(-1, width)
        picked = call(
            functools.partial(pick_kernel, n_y=n_y, strip=strip),
            shape((n_y, kmax, width), BF16),
            [VMEM(), VMEM()],
        )(ring, solved)
        got = exchange(picked, "y")
        return jnp.zeros_like(sent), jnp.sum(got.astype(F32), axis=0).astype(BF16)

    got, other = lax.cond(over[0, 0] > 0, by_rings, by_slots)
    leaf_solution = call(
        finish_kernel,
        shape((leaf_rows, width), F32),
        [SMEM()] * 2 + [VMEM()] * 7,
        [pltpu.VMEM((2 * kmax, width), BF16)],
    )(
        boundary_count,
        over,
        near(slots),
        near(got),
        near(other),
        near(taken),
        near(same),
        near(base),
        near(reach),
    )
    return leaf_solution[None, None], own[None]


def solution(mesh):
    n_leaf, n_sep = mesh.shape["leaf"], mesh.shape["sep"]
    n_y = 8
    torus = Mesh(mesh.devices.reshape(n_leaf // n_y // 2, 2, n_y, n_sep), ("zh", "zl", "y", "sep"))
    leaf = ("zh", "zl", "y")
    placed = (
        P(leaf, "sep", None, None),
        P(leaf, "sep", None, None, None, None),
        P(leaf, "sep", None, None),
        P(leaf, "sep", None),
        P(leaf, "sep", None),
        P(leaf, "sep"),
        P("sep", leaf, None),
        P(None, leaf, "sep", None, None),
        P(None, leaf, "sep", None),
    )
    return jax.shard_map(
        body,
        mesh=torus,
        in_specs=placed,
        out_specs=(P(leaf, "sep", None, None), P("sep", leaf, None)),
        check_vma=False,
    )
```

```python
import functools

import jax
import jax.numpy as jnp
from jax import lax
from jax.experimental import pallas as pl
from jax.experimental.pallas import tpu as pltpu
from jax.sharding import Mesh, PartitionSpec as P

TILE = 128
SHIFT = 7
DEAD = 255
SLOTS = 8
EXTRA = 8
F32 = jnp.float32
BF16 = jnp.bfloat16

SMEM = functools.partial(pl.BlockSpec, memory_space=pltpu.SMEM)
VMEM = functools.partial(pl.BlockSpec, memory_space=pltpu.VMEM)


def near(value):
    return pltpu.with_memory_space_constraint(value, pltpu.VMEM)


def call(kernel, out_shape, in_specs, scratch=(), out_specs=None):
    single = not isinstance(out_shape, (tuple, list))
    if out_specs is None:
        out_specs = VMEM() if single else tuple(VMEM() for _ in out_shape)
    return pl.pallas_call(
        kernel,
        out_shape=out_shape,
        in_specs=in_specs,
        out_specs=out_specs,
        scratch_shapes=list(scratch),
    )


def exchange(value, axes):
    return lax.all_to_all(value, axes, split_axis=0, concat_axis=0, tiled=True)


def over_rows(left, right):
    return lax.dot_general(left, right, (((0,), (0,)), ((), ())), preferred_element_type=F32)


def over_lanes(left, right):
    return lax.dot_general(left, right, (((1,), (1,)), ((), ())), preferred_element_type=F32)


def forward_kernel(
    cols, rows, targets, count, shots, tiles, own_map,
    forward, sent, taken, slots,
    rounded, exact, picked, filled, *, strip,
):
    count_rows, per_row = tiles.shape[0], tiles.shape[1]
    peers, _, width = sent.shape
    kmax = taken.shape[0]
    rounded[...] = shots[...].astype(BF16)
    for t in range(count_rows):
        total = None
        for k in range(0, per_row, 2):
            left = jnp.concatenate([tiles[t, k], tiles[t, k + 1]], axis=1)
            starts = [pl.multiple_of(cols[k + i, t] * TILE, TILE) for i in range(2)]
            right = jnp.concatenate([rounded[pl.ds(s, TILE), :] for s in starts], axis=0)
            term = jnp.dot(left, right, preferred_element_type=F32)
            total = term if total is None else total + term
        exact[pl.ds(t * TILE, TILE), :] = total
        forward[pl.ds(t * TILE, TILE), :] = total.astype(BF16)
    live = count[0, 0]
    for s in range(filled.shape[0]):
        filled[s] = 0
    lane = lax.broadcasted_iota(jnp.int32, own_map.shape, 1)
    place = jnp.zeros(own_map.shape, jnp.int32)
    most = 0
    for k in range(kmax):
        row = exact[pl.ds(rows[0, k], 1), :]
        taken[pl.ds(k, 1), :] = row
        picked[pl.ds(k, 1), :] = jnp.where(k < live, row, 0.0)
        owner = targets[0, k] // strip
        slot = filled[owner]
        alive = (k < live).astype(jnp.int32)
        filled[owner] = slot + alive
        most = jnp.maximum(most, alive * (slot + 1))
        place = jnp.where(lane == k, slot, place)
    target = own_map[...]
    slots[...] = jnp.where(lane < live, (target // strip) * SLOTS + jnp.minimum(place, SLOTS - 1), -1)
    high = jnp.where(lane < live, target >> SHIFT, DEAD).astype(F32)
    low = (target & (TILE - 1)).astype(F32)
    picked[pl.ds(kmax, EXTRA), :] = jnp.zeros((EXTRA, width), F32)
    picked[pl.ds(kmax, 1), pl.ds(0, kmax)] = high
    picked[pl.ds(kmax + 1, 1), pl.ds(0, kmax)] = low
    picked[pl.ds(kmax + 2, 1), pl.ds(0, kmax)] = place.astype(F32)
    over = jnp.where(most > SLOTS, 1.0, 0.0)
    picked[pl.ds(kmax + 3, 1), :] = jnp.full((1, width), over, F32)
    whole = picked[...].astype(BF16)
    for p in range(peers):
        sent[p] = whole


def ring_targets(got, n_rows, n_y, strip):
    y = lax.axis_index("y")
    kmax = got.shape[1] - EXTRA
    r = lax.broadcasted_iota(jnp.int32, (n_rows, kmax), 0)
    row_id = ((r // strip) * n_y + y) * strip + r % strip
    row_id = row_id.astype(F32)
    for p in range(got.shape[0]):
        info = got[p, pl.ds(kmax, EXTRA), :].astype(F32)
        target = info[0:1, :kmax] * float(TILE) + info[1:2, :kmax]
        yield p, info, jnp.where(row_id == target, 1.0, 0.0).astype(BF16)


def combine_kernel(got, load, cols, sent, summed, notes, *, n_y, strip):
    peers, _, width = got.shape
    n_z, _, half = sent.shape
    n_rows = n_z * strip
    kmax = got.shape[1] - EXTRA
    total, asked, over = None, None, None
    for p, info, hot in ring_targets(got, n_rows, n_y, strip):
        term = jnp.dot(hot, got[p, pl.ds(0, kmax), :], preferred_element_type=F32)
        total = term if total is None else total + term
        slot = lax.broadcasted_iota(jnp.int32, (TILE, kmax), 0)
        place = info[2:3, :kmax].astype(jnp.int32)
        mine = jnp.where(slot == place + p * SLOTS, 1.0, 0.0)
        mine = jnp.where(place < SLOTS, mine, 0.0).astype(BF16)
        wanted = over_lanes(hot, mine)
        asked = wanted if asked is None else asked + wanted
        flag = info[3:4, :TILE]
        over = flag if over is None else jnp.maximum(over, flag)
    rank = lax.broadcasted_iota(jnp.int32, (strip, TILE), 0).astype(F32) + 1.0
    lane = lax.broadcasted_iota(jnp.int32, over.shape, 1)
    notes[...] = jnp.zeros_like(notes)
    notes[pl.ds(EXTRA // 2, cols.shape[0]), pl.ds(0, cols.shape[1])] = cols[...].astype(F32)
    summed[...] = -total
    z = lax.axis_index("zh") * 2 + lax.axis_index("zl")
    own = pl.ds(pl.multiple_of(z * strip, strip), strip)
    summed[own, :] = summed[own, :] + load[...]
    halves = [summed[:, pl.ds(h * half, half)].astype(BF16) for h in range(2)]
    for p in range(n_z):
        sent[p, pl.ds(0, n_rows), :] = halves[p % 2]
        row = jnp.sum(asked[p * strip : (p + 1) * strip] * rank, axis=0, keepdims=True)
        notes[pl.ds(0, 1), :] = jnp.where(lane < peers * SLOTS, row, over)
        sent[p, pl.ds(n_rows, EXTRA), :] = notes[...].astype(BF16)


def residual_kernel(got, sent):
    n_rows = sent.shape[1]
    total = got[0, pl.ds(0, n_rows), :].astype(F32)
    for p in range(1, got.shape[0]):
        total = total + got[p, pl.ds(0, n_rows), :].astype(F32)
    value = total.astype(BF16)
    for p in range(sent.shape[0]):
        sent[p] = value


def separator_kernel(cols, near_cols, strips, near_strips, residual, got, product):
    per_row, sections = cols.shape
    n_y, n_rows, half = residual.shape
    strip = product.shape[1] - EXTRA
    per_tile = TILE // strip
    zl = lax.axis_index("zl")

    own_cols, other_cols = cols[...], near_cols[...]

    def tile(c):
        parts = n_y // per_tile
        y = (c % parts) * per_tile
        at = pl.multiple_of((c // parts) * strip, strip)
        return residual[pl.ds(y, per_tile), pl.ds(at, strip), :].reshape(TILE, half)

    over = got[0, pl.ds(n_rows, EXTRA), :].astype(F32)
    for p in range(1, got.shape[0]):
        over = jnp.maximum(over, got[p, pl.ds(n_rows, EXTRA), :].astype(F32))
    for which, wanted, rows in ((zl, own_cols, strips), (1 - zl, other_cols, near_strips)):
        for q in range(sections):
            total = None
            for k in range(0, per_row, 2):
                right = jnp.concatenate([tile(wanted[k, q]), tile(wanted[k + 1, q])], axis=0)
                left = rows[q, pl.ds(0, strip), pl.ds(k * TILE, 2 * TILE)]
                term = jnp.dot(left, right, preferred_element_type=F32)
                total = term if total is None else total + term
            product[which * sections + q, pl.ds(0, strip), :] = total
            product[which * sections + q, pl.ds(strip, EXTRA), :] = over


def solution_kernel(got, asked, own, sent, over):
    strip, width = own.shape
    half = got.shape[2]
    sections = got.shape[0] // 2
    most = None
    for h in range(2):
        total = None
        for p in range(h * sections, (h + 1) * sections):
            term = got[p, pl.ds(0, strip), :]
            total = term if total is None else total + term
            flag = got[p, pl.ds(strip, EXTRA), :]
            most = flag if most is None else jnp.maximum(most, flag)
        own[:, pl.ds(h * half, half)] = total
    lane = lax.broadcasted_iota(jnp.int32, most.shape, 1)
    over[0, 0] = (jnp.max(jnp.where(lane == TILE - 1, most, 0.0)) > 0.0).astype(jnp.int32)
    value = own[...].astype(BF16)
    n_z, held, _ = asked.shape
    per = sent.shape[0] // n_z
    rank = lax.broadcasted_iota(jnp.int32, (strip, TILE), 0).astype(F32) + 1.0
    for p in range(n_z):
        row = asked[p, pl.ds(held - EXTRA, EXTRA), :].astype(F32)[0:1]
        hot = jnp.where(rank == row, 1.0, 0.0).astype(BF16)
        rows = over_rows(hot, value)[: per * SLOTS]
        sent[pl.ds(p * per, per)] = rows.astype(BF16).reshape(per, SLOTS, width)


def pick_kernel(got, strips, sent, *, n_y, strip):
    n_rows = strips.shape[0]
    for p, _, hot in ring_targets(got, n_rows, n_y, strip):
        sent[p] = over_rows(hot, strips[...]).astype(BF16)


def transposed_kernel(cols, count, forward, tiles, row_lanes, base, reach, same, wide):
    count_rows, per_row = tiles.shape[0], tiles.shape[1]
    leaf_rows, width = forward.shape
    kmax = same.shape[0]
    wide[...] = jnp.zeros_like(wide)
    lanes = row_lanes[...]
    sums = None
    for t in range(count_rows):
        r = lax.broadcasted_iota(jnp.int32, (TILE, TILE), 0) + t * TILE
        hot = jnp.where(r == lanes, 1.0, 0.0).astype(BF16)
        term = over_rows(hot, hot)
        sums = term if sums is None else sums + term
        block = jnp.concatenate([forward[pl.ds(t * TILE, TILE), :], hot], axis=1)
        for k in range(per_row):
            at = pl.ds(pl.multiple_of(cols[k, t] * TILE, TILE), TILE)
            wide[at, :] = wide[at, :] + over_rows(tiles[t, k], block)
    base[...] = wide[:, pl.ds(0, width)]
    reach[...] = wide[:, pl.ds(width, TILE)].astype(BF16)
    same[...] = sums[:kmax]


def finish(needed, count, taken, same, base, reach, out, change):
    kmax = taken.shape[0]
    equal = same[...][:, :kmax]
    k = lax.broadcasted_iota(jnp.int32, equal.shape, 1)
    mine = lax.broadcasted_iota(jnp.int32, equal.shape, 0)
    earlier = jnp.sum(jnp.where(k < mine, equal, 0.0), axis=1, keepdims=True)
    live = jnp.where(k < count[0, 0], equal, 0.0).astype(BF16)
    term = jnp.dot(live, needed().astype(BF16), preferred_element_type=F32)
    before = taken[...]
    delta = (before - term).astype(BF16).astype(F32) - before.astype(BF16).astype(F32)
    delta = jnp.where(earlier == 0.0, delta, 0.0)
    high = delta.astype(BF16)
    change[pl.ds(0, kmax), :] = high
    change[pl.ds(kmax, kmax), :] = (delta - high.astype(F32)).astype(BF16)
    out[...] = base[...] + jnp.dot(reach[...], change[...], preferred_element_type=F32)


def finish_kernel(count, over, slots, got, other, taken, same, base, reach, out, change):
    def needed():
        n_leaf, per, width = got.shape
        rows = got[...].reshape(n_leaf * per, width)
        at = lax.broadcasted_iota(jnp.int32, (n_leaf * per, slots.shape[1]), 0)
        hot = jnp.where(at == slots[...], 1.0, 0.0).astype(BF16)
        return jnp.where(over[0, 0] > 0, other[...].astype(F32), over_rows(hot, rows))

    finish(needed, count, taken, same, base, reach, out, change)


def body(
    shot_columns,
    factor_tiles,
    factor_cols,
    boundary_rows,
    boundary_map,
    boundary_count,
    separator_load,
    inverse_tiles,
    inverse_cols,
):
    z_axes = ("zh", "zl")
    n_z, n_y = lax.axis_size(z_axes), lax.axis_size("y")
    n_sep, n_leaf = lax.axis_size("sep"), n_z * n_y
    shots, tiles, cols = shot_columns[0, 0], factor_tiles[0, 0], factor_cols[0, 0].T
    rows, own_map, load = boundary_rows[0], boundary_map[0], separator_load[0]
    leaf_rows, width = shots.shape
    kmax = rows.shape[1]
    strip = load.shape[0]
    shape = jax.ShapeDtypeStruct
    tile_cols = inverse_cols[:, 0, 0].T
    strips = inverse_tiles[:, :, 0].reshape(n_sep, strip, -1)
    near_strips = lax.ppermute(strips, "zl", [(0, 1), (1, 0)])
    forward, sent, taken, slots = call(
        functools.partial(forward_kernel, strip=strip),
        (
            shape((leaf_rows, width), BF16),
            shape((n_y, kmax + EXTRA, width), BF16),
            shape((kmax, width), F32),
            shape((1, kmax), jnp.int32),
        ),
        [SMEM(), SMEM(), SMEM(), SMEM(), VMEM(), VMEM(), VMEM()],
        [
            pltpu.VMEM((leaf_rows, width), BF16),
            pltpu.VMEM((leaf_rows, width), F32),
            pltpu.VMEM((kmax + EXTRA, width), F32),
            pltpu.SMEM((n_leaf,), jnp.int32),
        ],
    )(cols, rows, own_map, boundary_count, shots, tiles, own_map)
    ring = exchange(sent, "y")
    half = width // 2
    sent = call(
        functools.partial(combine_kernel, n_y=n_y, strip=strip),
        shape((n_z, n_z * strip + EXTRA, half), BF16),
        [VMEM(), VMEM(), VMEM()],
        [pltpu.VMEM((n_z * strip, width), F32), pltpu.VMEM((EXTRA, half), F32)],
    )(near(ring), near(load), near(tile_cols))
    asked = exchange(sent, z_axes)
    beside = lax.axis_index("zh") * 2 + 1 - lax.axis_index("zl")
    near_cols = lax.dynamic_slice(
        asked, (beside, n_z * strip + EXTRA // 2, 0), (1,) + tile_cols.shape
    )[0].astype(jnp.int32)
    sent = call(residual_kernel, shape((n_y, n_z * strip, half), BF16), [VMEM()])(near(asked))
    residual = exchange(sent, "y")
    held_rows, _ = lax.optimization_barrier((rows, asked[0, 0, 0]))
    base, reach, same = call(
        transposed_kernel,
        (
            pltpu.VMEM((leaf_rows, width), F32),
            pltpu.VMEM((leaf_rows, TILE), BF16),
            shape((kmax, TILE), F32),
        ),
        [SMEM(), SMEM(), VMEM(), VMEM(), VMEM()],
        [pltpu.VMEM((leaf_rows, width + TILE), F32)],
    )(cols, boundary_count, forward, tiles, jnp.concatenate([held_rows, held_rows], axis=1))
    product = call(
        separator_kernel,
        shape((2 * n_sep, strip + EXTRA, half), F32),
        [VMEM()] * 6,
    )(near(tile_cols), near(near_cols), near(strips), near(near_strips), near(residual), near(asked))
    got = exchange(product, ("zl", "sep"))
    own, sent, over = call(
        solution_kernel,
        (shape((strip, width), F32), shape((n_leaf, SLOTS, width), BF16), shape((1, 1), jnp.int32)),
        [VMEM(), VMEM()],
        out_specs=(VMEM(), VMEM(), SMEM()),
    )(near(got), near(asked))

    def by_slots():
        return exchange(sent, z_axes + ("y",)), jnp.zeros((kmax, width), BF16)

    def by_rings():
        value = jnp.broadcast_to(own.astype(BF16)[None], (n_z, strip, width))
        solved = exchange(value, z_axes).reshape(-1, width)
        picked = call(
            functools.partial(pick_kernel, n_y=n_y, strip=strip),
            shape((n_y, kmax, width), BF16),
            [VMEM(), VMEM()],
        )(ring, solved)
        got = exchange(picked, "y")
        return jnp.zeros_like(sent), jnp.sum(got.astype(F32), axis=0).astype(BF16)

    got, other = lax.cond(over[0, 0] > 0, by_rings, by_slots)
    leaf_solution = call(
        finish_kernel,
        shape((leaf_rows, width), F32),
        [SMEM()] * 2 + [VMEM()] * 7,
        [pltpu.VMEM((2 * kmax, width), BF16)],
    )(
        boundary_count,
        over,
        near(slots),
        near(got),
        near(other),
        near(taken),
        near(same),
        near(base),
        near(reach),
    )
    return leaf_solution[None, None], own[None]


def solution(mesh):
    n_leaf, n_sep = mesh.shape["leaf"], mesh.shape["sep"]
    n_y = 8
    torus = Mesh(mesh.devices.reshape(n_leaf // n_y // 2, 2, n_y, n_sep), ("zh", "zl", "y", "sep"))
    leaf = ("zh", "zl", "y")
    placed = (
        P(leaf, "sep", None, None),
        P(leaf, "sep", None, None, None, None),
        P(leaf, "sep", None, None),
        P(leaf, "sep", None),
        P(leaf, "sep", None),
        P(leaf, "sep"),
        P("sep", leaf, None),
        P(None, leaf, "sep", None, None),
        P(None, leaf, "sep", None),
    )
    return jax.shard_map(
        body,
        mesh=torus,
        in_specs=placed,
        out_specs=(P(leaf, "sep", None, None), P("sep", leaf, None)),
        check_vma=False,
    )
```
